256 devices in a mesh: space: 16 (over z, x_hi), band: 16 (over y, x_lo, core).
Axes of the slice: x: 4 (x_hi: 2, x_lo: 2; x = x_hi * 2 + x_lo), y: 4, z: 8, core: 2. Of those that a mesh axis runs over, the one named last changes fastest.
Arguments:
- orbitals: float32 [192, 512, 256], P('space', 'band'), may hold values from -6 to 6
- potential: float32 [192, 256], P('space'), may hold values from -10 to 10
Outputs:
- rotated: float32 [192, 512, 256], P('space', 'band')
- correlation: float32 [512, 512], replicated
The draws below stay inside these ranges and needn't reach their ends.
All inputs are finite; a program needn't handle non-finite values.
Results may differ from the reference program's by a relative error of at most 0.000098.
Values sent between devices are 32-bit elements; how exact they have to be, the bound alone decides.
No kernel may reach another device: no remote copies, remote signals or barrier semaphores. Data moves between devices by JAX's collectives and lax.ppermute only.
A program may use at most 320 MiB of HBM per device.

```python
import jax
import jax.numpy as jnp
from jax import lax

NX = 16
NY = 16
NB = 512
NZ = 192


def draw_orbitals(key, part):
    cells = NX * NY
    shared = jax.random.truncated_normal(jax.random.fold_in(key, 2), -4.0, 4.0, (NZ, 1, cells), jnp.float32)
    signs = 2.0 * jax.random.randint(jax.random.fold_in(key, 3), (1, NB, 1), 0, 2).astype(jnp.float32) - 1.0
    noise = jax.random.truncated_normal(jax.random.fold_in(key, 1), -4.0, 4.0, (NZ, NB, cells), jnp.float32)
    amount = 1.0 / 3.0
    return noise + amount * signs * shared


def level_of(rng, shape, pieces, smallest, high):
    level, own = 1.0, jax.random.fold_in(rng, 6)
    for position, shards_of in pieces:
        draws = jnp.exp(jax.random.uniform(jax.random.fold_in(own, position), (shards_of,), jnp.float32, smallest / len(pieces), high / len(pieces)))
        level = level * jnp.repeat(draws, shape[position] // shards_of).reshape([-1 if axis == position else 1 for axis in range(len(shape))])
    return level


def setup_inputs(seed: int = 0) -> dict:
    streams_of = jax.random.split(jax.random.key(seed), 3)
    return {
        "orbitals": draw_orbitals(jax.random.fold_in(streams_of[2], 71), 0),
        "potential": jnp.clip(jax.random.uniform(streams_of[1], (NZ, NX * NY), jnp.float32, -10.0, 10.0) * level_of(streams_of[1], (NZ, NX * NY), ((0, 16),), -0.4, 0.0), -10.0, 10.0),
    }


COEFS = [12.0 / 7.0, -15.0 / 56.0, 10.0 / 189.0, -1.0 / 112.0, 2.0 / 1925.0, -1.0 / 16632.0]
CENTER_COEF = -5369.0 / 1800.0
INV_SPACING2 = 6.25
SHIFT_MID = 42.0
HALF_SPAN = 38.0

def operate(field, potential):
    grid = field.reshape(NZ, NB, NX, NY)
    lap = 3.0 * CENTER_COEF * grid
    for k in range(6):
        for axis_num in (0, 2, 3):
            lap = lap + COEFS[k] * (jnp.roll(grid, k + 1, axis_num) + jnp.roll(grid, -(k + 1), axis_num))
    lap = lap.reshape(field.shape)
    return -0.5 * INV_SPACING2 * lap + potential[:, None, :] * field

def reference(orbitals, potential):
    first = (operate(orbitals, potential) - SHIFT_MID * orbitals) / HALF_SPAN
    second = 2.0 * (operate(first, potential) - SHIFT_MID * first) / HALF_SPAN - orbitals
    gram = jnp.einsum('zig,zjg->ij', second, second, precision=lax.Precision.HIGHEST)
    correlation = gram / float(NX * NY * NZ)
    lower = jnp.linalg.cholesky(correlation)
    ident = jnp.eye(NB, dtype=jnp.float32)
    factor = jax.scipy.linalg.solve_triangular(lower, ident, lower=True).T
    rotated = jnp.einsum('zig,ij->zjg', second, factor, precision=lax.Precision.HIGHEST)
    return (rotated, correlation)
```

```python
import functools

import jax
import jax.numpy as jnp
import numpy as np
from jax import lax
from jax.experimental import pallas as pl
from jax.experimental.pallas import tpu as pltpu
from jax.sharding import Mesh
from jax.sharding import PartitionSpec as P

NX = 16
NY = 16
CELLS = NX * NY
COEFS = [12.0 / 7.0, -15.0 / 56.0, 10.0 / 189.0, -1.0 / 112.0, 2.0 / 1925.0, -1.0 / 16632.0]
CENTER_COEF = -5369.0 / 1800.0
INV_SPACING2 = 6.25
SHIFT_MID = 42.0
HALF_SPAN = 38.0
RADIUS = 6

SPACE = ("z", "xh")
TEAM = ("y", "xl")
BAND = ("y", "xl", "c")

BLOCKS = [[(0, 0), (1, 0), (1, 1), (2, 0), (2, 1)], [(2, 2), (3, 0), (3, 1), (3, 2), (3, 3)]]
TILE = 128

SCALE = -0.5 * INV_SPACING2 / HALF_SPAN


def plane_matrix():
    ring = np.zeros((NX, NX))
    for k, coef in enumerate(COEFS):
        for i in range(NX):
            ring[i, (i + k + 1) % NX] += coef
            ring[i, (i - k - 1) % NX] += coef
    one = np.eye(NX)
    full = np.kron(ring, one) + np.kron(one, ring) + 3.0 * CENTER_COEF * np.eye(CELLS)
    return (SCALE * full).astype(np.float32)


def dot32(a, b, dims):
    return lax.dot_general(
        a, b, (dims, ((), ())), precision=lax.Precision.HIGHEST, preferred_element_type=jnp.float32
    )


def filter_kernel(rows, planes, low, own, pot, high, mat, out, first):
    def field(p):
        if p < planes:
            return low[p * rows : (p + 1) * rows, :]
        if p < 2 * planes:
            return own[(p - planes) * rows : (p - planes + 1) * rows, :]
        return high[(p - 2 * planes) * rows : (p - 2 * planes + 1) * rows, :]

    def level(p):
        if p < planes:
            row = low[planes * rows + p : planes * rows + p + 1, :]
        elif p < 2 * planes:
            row = pot[p - planes : p - planes + 1, :]
        else:
            row = high[planes * rows + p - 2 * planes : planes * rows + p - 2 * planes + 1, :]
        return (row - SHIFT_MID) / HALF_SPAN

    half = RADIUS * rows
    first[0:half, :] = dot32(low[(planes - RADIUS) * rows : planes * rows, :], mat[...], ((1,), (0,)))
    first[half : half + planes * rows, :] = dot32(own[...], mat[...], ((1,), (0,)))
    first[half + planes * rows :, :] = dot32(high[0:half, :], mat[...], ((1,), (0,)))
    for q in range(planes + 2 * RADIUS):
        p = q + planes - RADIUS
        acc = first[q * rows : (q + 1) * rows, :] + level(p) * field(p)
        for k in range(RADIUS):
            acc = acc + (SCALE * COEFS[k]) * (field(p + k + 1) + field(p - k - 1))
        first[q * rows : (q + 1) * rows, :] = acc
    inner = dot32(first[half : half + planes * rows, :], mat[...], ((1,), (0,)))
    for z in range(planes):
        q = z + RADIUS
        centre = first[q * rows : (q + 1) * rows, :]
        acc = inner[z * rows : (z + 1) * rows, :] + level(z + planes) * centre
        for k in range(RADIUS):
            up = first[(q + k + 1) * rows : (q + k + 2) * rows, :]
            down = first[(q - k - 1) * rows : (q - k) * rows, :]
            acc = acc + (SCALE * COEFS[k]) * (up + down)
        second = 2.0 * acc - field(z + planes)
        out[2 * z] = second[:, :TILE]
        out[2 * z + 1] = second[:, TILE:]


def gram_kernel(scale, core, own, other, out, stack):
    c = core[0]
    rows = own.shape[2]
    for half, ref in ((c, own), (1 - c, other)):
        for s in range(own.shape[0]):
            for t in range(own.shape[1]):
                at = pl.multiple_of(s * 2 * rows + half * rows, rows)
                stack[pl.ds(at, rows), t * TILE : (t + 1) * TILE] = ref[s, t]
    for k in range(5):
        i = jnp.where(c == 0, BLOCKS[0][k][0], BLOCKS[1][k][0])
        j = jnp.where(c == 0, BLOCKS[0][k][1], BLOCKS[1][k][1])
        a = stack[pl.ds(pl.multiple_of(i * TILE, TILE), TILE), :]
        b = stack[pl.ds(pl.multiple_of(j * TILE, TILE), TILE), :]
        out[k * TILE : (k + 1) * TILE, :] = dot32(a, b, ((1,), (1,))) * scale


def join_kernel(core, own, other, out):
    first = core[0] == 0
    for k in range(5):
        rows = slice(k * TILE, (k + 1) * TILE)
        a, b = own[rows, :], other[rows, :]
        for blocks, block in ((BLOCKS[0], jnp.where(first, a, b)), (BLOCKS[1], jnp.where(first, b, a))):
            i, j = blocks[k]
            out[i * TILE : (i + 1) * TILE, j * TILE : (j + 1) * TILE] = block
            if i != j:
                out[j * TILE : (j + 1) * TILE, i * TILE : (i + 1) * TILE] = block.T


def rotate_kernel(weights, fields, out):
    for t in range(fields.shape[0] // 2):
        for h in range(2):
            out[t, :, h * TILE : (h + 1) * TILE] = dot32(
                weights[...], fields[2 * t + h], ((1,), (0,))
            )


VMEM = pl.BlockSpec(memory_space=pltpu.VMEM)
SMEM = pl.BlockSpec(memory_space=pltpu.SMEM)
PARAMS = pltpu.CompilerParams(vmem_limit_bytes=48 << 20)


def ring(axes, step):
    count = lax.axis_size(axes)
    return [(i, (i + step) % count) for i in range(count)]


def flip(axes, bits):
    return [(i, i ^ bits) for i in range(lax.axis_size(axes))]


def per_device(orbitals, potential):
    planes, rows, cells = orbitals.shape
    core = lax.axis_index("c").astype(jnp.int32).reshape(1)
    own = orbitals.reshape(planes * rows, cells)
    packed = jnp.concatenate([own, potential], axis=0)
    low = lax.ppermute(packed, SPACE, ring(SPACE, 1))
    high = lax.ppermute(packed, SPACE, ring(SPACE, -1))
    second = pl.pallas_call(
        functools.partial(filter_kernel, rows, planes),
        out_shape=jax.ShapeDtypeStruct((2 * planes, rows, TILE), jnp.float32),
        in_specs=[VMEM] * 5,
        out_specs=VMEM,
        scratch_shapes=[pltpu.VMEM(((planes + 2 * RADIUS) * rows, cells), jnp.float32)],
        compiler_params=PARAMS,
        name="filter",
    )(low, own, potential, high, jnp.asarray(plane_matrix()))

    team = lax.axis_size(TEAM)
    mine = lax.all_to_all(second.reshape(team, 2 * planes // team, rows, TILE), TEAM, 0, 0)
    theirs = lax.ppermute(mine, ("c",), flip("c", 1))
    count = 2 * team * rows
    total = float(planes * lax.axis_size(SPACE) * cells)
    part = pl.pallas_call(
        functools.partial(gram_kernel, 1.0 / total),
        out_shape=jax.ShapeDtypeStruct((5 * TILE, TILE), jnp.float32),
        in_specs=[SMEM, VMEM, VMEM],
        out_specs=VMEM,
        scratch_shapes=[pltpu.VMEM((count, mine.shape[1] * TILE), jnp.float32)],
        compiler_params=PARAMS,
        name="gram",
    )(core, mine, theirs)

    piece = lax.all_to_all(part.reshape(team, 5 * TILE // team, TILE), TEAM, 0, 0).sum(0)
    for bits in ((1, 2, 3), (4, 8, 12)):
        got = [lax.ppermute(piece, SPACE, flip(SPACE, b)) for b in bits]
        piece = (piece + got[0]) + (got[1] + got[2])
    spread = lax.all_to_all(jnp.broadcast_to(piece, (team,) + piece.shape), TEAM, 0, 0)
    mine_g = spread.reshape(5 * TILE, TILE)
    theirs_g = lax.ppermute(mine_g, ("c",), flip("c", 1))
    correlation = pl.pallas_call(
        join_kernel,
        out_shape=jax.ShapeDtypeStruct((count, count), jnp.float32),
        in_specs=[SMEM, VMEM, VMEM],
        out_specs=VMEM,
        compiler_params=PARAMS,
        name="join",
    )(core, mine_g, theirs_g)
    lower = jnp.linalg.cholesky(correlation)
    ident = jnp.eye(count, dtype=jnp.float32)
    inverse = jax.scipy.linalg.solve_triangular(lower, ident, lower=True)
    weights = lax.dynamic_slice_in_dim(inverse, lax.axis_index(BAND) * rows, rows, 0)

    fields = lax.all_gather(second, BAND, axis=1, tiled=True)
    steps = 4
    rotated = pl.pallas_call(
        rotate_kernel,
        out_shape=jax.ShapeDtypeStruct((planes, rows, cells), jnp.float32),
        grid=(steps,),
        in_specs=[
            pl.BlockSpec((rows, count), lambda i: (0, 0)),
            pl.BlockSpec((2 * planes // steps, count, TILE), lambda i: (i, 0, 0)),
        ],
        out_specs=pl.BlockSpec((planes // steps, rows, cells), lambda i: (i, 0, 0)),
        compiler_params=PARAMS,
        name="rotate",
    )(weights, fields)
    return (rotated, correlation)


def solution(mesh):
    fine = Mesh(mesh.devices.reshape(8, 2, 4, 2, 2), ("z", "xh", "y", "xl", "c"))
    return jax.shard_map(
        per_device,
        mesh=fine,
        in_specs=(P(SPACE, BAND, None), P(SPACE, None)),
        out_specs=(P(SPACE, BAND, None), P()),
        check_vma=False,
    )
```

```python
import functools

import jax
import jax.numpy as jnp
import numpy as np
from jax import lax
from jax.experimental import pallas as pl
from jax.experimental.pallas import tpu as pltpu
from jax.sharding import Mesh
from jax.sharding import PartitionSpec as P

NX = 16
NY = 16
CELLS = NX * NY
COEFS = [12.0 / 7.0, -15.0 / 56.0, 10.0 / 189.0, -1.0 / 112.0, 2.0 / 1925.0, -1.0 / 16632.0]
CENTER_COEF = -5369.0 / 1800.0
INV_SPACING2 = 6.25
SHIFT_MID = 42.0
HALF_SPAN = 38.0
RADIUS = 6

SPACE = ("z", "xh")
TEAM = ("y", "xl")
BAND = ("y", "xl", "c")

BLOCKS = [[(0, 0), (1, 0), (1, 1), (2, 0), (2, 1)], [(2, 2), (3, 0), (3, 1), (3, 2), (3, 3)]]
TILE = 128
GROUP = 16

SCALE = -0.5 * INV_SPACING2 / HALF_SPAN


def plane_matrix():
    ring = np.zeros((NX, NX))
    for k, coef in enumerate(COEFS):
        for i in range(NX):
            ring[i, (i + k + 1) % NX] += coef
            ring[i, (i - k - 1) % NX] += coef
    one = np.eye(NX)
    full = np.kron(ring, one) + np.kron(one, ring) + 3.0 * CENTER_COEF * np.eye(CELLS)
    return (SCALE * full).astype(np.float32)


def dot32(a, b, dims):
    return lax.dot_general(
        a, b, (dims, ((), ())), precision=lax.Precision.HIGHEST, preferred_element_type=jnp.float32
    )


def filter_kernel(rows, planes, low, own, pot, high, mat, out, first):
    def field(p):
        if p < planes:
            return low[p * rows : (p + 1) * rows, :]
        if p < 2 * planes:
            return own[(p - planes) * rows : (p - planes + 1) * rows, :]
        return high[(p - 2 * planes) * rows : (p - 2 * planes + 1) * rows, :]

    def level(p):
        if p < planes:
            row = low[planes * rows + p : planes * rows + p + 1, :]
        elif p < 2 * planes:
            row = pot[p - planes : p - planes + 1, :]
        else:
            row = high[planes * rows + p - 2 * planes : planes * rows + p - 2 * planes + 1, :]
        return (row - SHIFT_MID) / HALF_SPAN

    half = RADIUS * rows
    first[0:half, :] = dot32(low[(planes - RADIUS) * rows : planes * rows, :], mat[...], ((1,), (0,)))
    first[half : half + planes * rows, :] = dot32(own[...], mat[...], ((1,), (0,)))
    first[half + planes * rows :, :] = dot32(high[0:half, :], mat[...], ((1,), (0,)))
    for q in range(planes + 2 * RADIUS):
        p = q + planes - RADIUS
        acc = first[q * rows : (q + 1) * rows, :] + level(p) * field(p)
        for k in range(RADIUS):
            acc = acc + (SCALE * COEFS[k]) * (field(p + k + 1) + field(p - k - 1))
        first[q * rows : (q + 1) * rows, :] = acc
    inner = dot32(first[half : half + planes * rows, :], mat[...], ((1,), (0,)))
    for z in range(planes):
        q = z + RADIUS
        centre = first[q * rows : (q + 1) * rows, :]
        acc = inner[z * rows : (z + 1) * rows, :] + level(z + planes) * centre
        for k in range(RADIUS):
            up = first[(q + k + 1) * rows : (q + k + 2) * rows, :]
            down = first[(q - k - 1) * rows : (q - k) * rows, :]
            acc = acc + (SCALE * COEFS[k]) * (up + down)
        second = 2.0 * acc - field(z + planes)
        out[2 * z] = second[:, :TILE]
        out[2 * z + 1] = second[:, TILE:]


def gram_kernel(scale, place, own, other, out, stack):
    c = place[0]
    rows = own.shape[2]
    for half, ref in ((c, own), (1 - c, other)):
        for s in range(own.shape[0]):
            for t in range(own.shape[1]):
                at = pl.multiple_of(s * 2 * rows + half * rows, rows)
                stack[pl.ds(at, rows), t * TILE : (t + 1) * TILE] = ref[s, t]
    for k in range(5):
        i = jnp.where(c == 0, BLOCKS[0][k][0], BLOCKS[1][k][0])
        j = jnp.where(c == 0, BLOCKS[0][k][1], BLOCKS[1][k][1])
        a = stack[pl.ds(pl.multiple_of(i * TILE, TILE), TILE), :]
        b = stack[pl.ds(pl.multiple_of(j * TILE, TILE), TILE), :]
        out[k * TILE : (k + 1) * TILE, :] = dot32(a, b, ((1,), (1,))) * scale


def line(block, row):
    return jnp.broadcast_to(block[row : row + 1, :], (8, TILE))


def factor_tile(ref, origin):
    lane = lax.broadcasted_iota(jnp.int32, (8, TILE), 1)
    sub = lax.broadcasted_iota(jnp.int32, (8, TILE), 0)
    lanes = slice(origin, origin + TILE)
    halves = range(GROUP // 8)
    for base in range(0, TILE, GROUP):
        inside = (lane >= base) & (lane < base + GROUP)
        place = [slice(origin + base + 8 * h, origin + base + 8 * h + 8) for h in halves]
        rows = [ref[place[h], lanes] for h in halves]
        col = [
            [jnp.broadcast_to(rows[h][:, base + k : base + k + 1], (8, TILE)) for k in range(GROUP)]
            for h in halves
        ]
        start = [
            jnp.where(inside, jnp.where(lane - base == sub + 8 * h, 1.0, 0.0), rows[h]) for h in halves
        ]
        low, full = list(start), list(start)
        scale = [jnp.zeros((8, TILE), jnp.float32) for _ in halves]
        for j in range(GROUP):
            h, r = divmod(j, 8)
            at = sub == r
            pivot = line(col[h][j], r)
            inv = 1.0 / pivot
            scale[h] = jnp.where(at, lax.rsqrt(pivot), scale[h])
            mine = [col[i][j] for i in halves]
            for k in range(j + 1, GROUP):
                ratio = line(col[h][k], r) * inv
                for i in halves:
                    new = col[i][k] - mine[i] * ratio
                    col[i][k] = jnp.where(at, ratio, new) if i == h else new
            ratio = line(low[h], r) * inv
            for i in range(h, GROUP // 8):
                low[i] = low[i] - (jnp.where(sub > r, mine[i], 0.0) if i == h else mine[i]) * ratio
            ratio = line(full[h], r) * inv
            for i in halves:
                new = full[i] - mine[i] * ratio
                full[i] = jnp.where(at, ratio, new) if i == h else new
        for h in halves:
            ref[place[h], lanes] = jnp.where(lane < base + GROUP, low[h] * scale[h], 0.0)
        for q in range(base + GROUP, TILE, 8):
            rest = ref[origin + q : origin + q + 8, lanes]
            acc = jnp.where(inside, 0.0, rest)
            for m in range(GROUP):
                acc = acc - jnp.broadcast_to(rest[:, base + m : base + m + 1], (8, TILE)) * line(
                    full[m // 8], m % 8
                )
            ref[origin + q : origin + q + 8, lanes] = acc


def factor_kernel(place, own, other, corr, weights, work):
    first = place[0] == 0
    for k in range(5):
        rows = slice(k * TILE, (k + 1) * TILE)
        a, b = own[rows, :], other[rows, :]
        for blocks, block in ((BLOCKS[0], jnp.where(first, a, b)), (BLOCKS[1], jnp.where(first, b, a))):
            i, j = blocks[k]
            corr[i * TILE : (i + 1) * TILE, j * TILE : (j + 1) * TILE] = block
            if i != j:
                corr[j * TILE : (j + 1) * TILE, i * TILE : (i + 1) * TILE] = block.T
    work[...] = corr[...]
    count = work.shape[0]
    for k in range(0, count, TILE):
        own_rows = slice(k, k + TILE)
        factor_tile(work, k)
        inverse = work[own_rows, own_rows]
        for side in (slice(0, k), slice(k + TILE, count)):
            if side.start < side.stop:
                work[own_rows, side] = dot32(inverse, work[own_rows, side], ((1,), (0,)))
        for r in range(k + TILE, count, TILE):
            rows = slice(r, r + TILE)
            lower = work[own_rows, rows].T
            for side in (slice(r, count), slice(0, k)):
                if side.start < side.stop:
                    work[rows, side] = work[rows, side] - dot32(lower, work[own_rows, side], ((1,), (0,)))
            work[rows, own_rows] = -dot32(lower, inverse, ((1,), (0,)))
    size = weights.shape[0]
    begin = pl.multiple_of(place[1] * size, size)
    limit = (place[1] * size // TILE + 1) * TILE
    column = lax.broadcasted_iota(jnp.int32, (size, count), 1)
    weights[...] = jnp.where(column < limit, work[pl.ds(begin, size), :], 0.0)


def rotate_kernel(weights, fields, out):
    for t in range(fields.shape[0] // 2):
        for h in range(2):
            out[t, :, h * TILE : (h + 1) * TILE] = dot32(
                weights[...], fields[2 * t + h], ((1,), (0,))
            )


VMEM = pl.BlockSpec(memory_space=pltpu.VMEM)
SMEM = pl.BlockSpec(memory_space=pltpu.SMEM)
PARAMS = pltpu.CompilerParams(vmem_limit_bytes=48 << 20)


def ring(axes, step):
    count = lax.axis_size(axes)
    return [(i, (i + step) % count) for i in range(count)]


def flip(axes, bits):
    return [(i, i ^ bits) for i in range(lax.axis_size(axes))]


def per_device(orbitals, potential):
    planes, rows, cells = orbitals.shape
    place = jnp.stack([lax.axis_index("c"), lax.axis_index(BAND)]).astype(jnp.int32)
    own = orbitals.reshape(planes * rows, cells)
    packed = jnp.concatenate([own, potential], axis=0)
    low = lax.ppermute(packed, SPACE, ring(SPACE, 1))
    high = lax.ppermute(packed, SPACE, ring(SPACE, -1))
    second = pl.pallas_call(
        functools.partial(filter_kernel, rows, planes),
        out_shape=jax.ShapeDtypeStruct((2 * planes, rows, TILE), jnp.float32),
        in_specs=[VMEM] * 5,
        out_specs=VMEM,
        scratch_shapes=[pltpu.VMEM(((planes + 2 * RADIUS) * rows, cells), jnp.float32)],
        compiler_params=PARAMS,
        name="filter",
    )(low, own, potential, high, jnp.asarray(plane_matrix()))

    team = lax.axis_size(TEAM)
    mine = lax.all_to_all(second.reshape(team, 2 * planes // team, rows, TILE), TEAM, 0, 0)
    theirs = lax.ppermute(mine, ("c",), flip("c", 1))
    count = 2 * team * rows
    total = float(planes * lax.axis_size(SPACE) * cells)
    part = pl.pallas_call(
        functools.partial(gram_kernel, 1.0 / total),
        out_shape=jax.ShapeDtypeStruct((5 * TILE, TILE), jnp.float32),
        in_specs=[SMEM, VMEM, VMEM],
        out_specs=VMEM,
        scratch_shapes=[pltpu.VMEM((count, mine.shape[1] * TILE), jnp.float32)],
        compiler_params=PARAMS,
        name="gram",
    )(place, mine, theirs)

    piece = lax.all_to_all(part.reshape(team, 5 * TILE // team, TILE), TEAM, 0, 0).sum(0)
    for bits in ((1, 2, 3), (4, 8, 12)):
        got = [lax.ppermute(piece, SPACE, flip(SPACE, b)) for b in bits]
        piece = (piece + got[0]) + (got[1] + got[2])
    spread = lax.all_to_all(jnp.broadcast_to(piece, (team,) + piece.shape), TEAM, 0, 0)
    mine_g = spread.reshape(5 * TILE, TILE)
    theirs_g = lax.ppermute(mine_g, ("c",), flip("c", 1))
    correlation, weights = pl.pallas_call(
        factor_kernel,
        out_shape=(
            jax.ShapeDtypeStruct((count, count), jnp.float32),
            jax.ShapeDtypeStruct((rows, count), jnp.float32),
        ),
        in_specs=[SMEM, VMEM, VMEM],
        out_specs=(VMEM, VMEM),
        scratch_shapes=[pltpu.VMEM((count, count), jnp.float32)],
        compiler_params=PARAMS,
        name="factor",
    )(place, mine_g, theirs_g)

    fields = lax.all_gather(second, BAND, axis=1, tiled=True)
    steps = 4
    rotated = pl.pallas_call(
        rotate_kernel,
        out_shape=jax.ShapeDtypeStruct((planes, rows, cells), jnp.float32),
        grid=(steps,),
        in_specs=[
            pl.BlockSpec((rows, count), lambda i: (0, 0)),
            pl.BlockSpec((2 * planes // steps, count, TILE), lambda i: (i, 0, 0)),
        ],
        out_specs=pl.BlockSpec((planes // steps, rows, cells), lambda i: (i, 0, 0)),
        compiler_params=PARAMS,
        name="rotate",
    )(weights, fields)
    return (rotated, correlation)


def solution(mesh):
    fine = Mesh(mesh.devices.reshape(8, 2, 4, 2, 2), ("z", "xh", "y", "xl", "c"))
    return jax.shard_map(
        per_device,
        mesh=fine,
        in_specs=(P(SPACE, BAND, None), P(SPACE, None)),
        out_specs=(P(SPACE, BAND, None), P()),
        check_vma=False,
    )
```

```python
import functools

import jax
import jax.numpy as jnp
import numpy as np
from jax import lax
from jax.experimental import pallas as pl
from jax.experimental.pallas import tpu as pltpu
from jax.sharding import Mesh
from jax.sharding import PartitionSpec as P

NX = 16
NY = 16
CELLS = NX * NY
COEFS = [12.0 / 7.0, -15.0 / 56.0, 10.0 / 189.0, -1.0 / 112.0, 2.0 / 1925.0, -1.0 / 16632.0]
CENTER_COEF = -5369.0 / 1800.0
INV_SPACING2 = 6.25
SHIFT_MID = 42.0
HALF_SPAN = 38.0
RADIUS = 6

SPACE = ("z", "xh")
TEAM = ("y", "xl")
BAND = ("y", "xl", "c")

BLOCKS = [[(0, 0), (1, 0), (1, 1), (2, 0), (2, 1)], [(2, 2), (3, 0), (3, 1), (3, 2), (3, 3)]]
TILE = 128
GROUP = 16

SCALE = -0.5 * INV_SPACING2 / HALF_SPAN


def plane_matrix():
    ring = np.zeros((NX, NX))
    for k, coef in enumerate(COEFS):
        for i in range(NX):
            ring[i, (i + k + 1) % NX] += coef
            ring[i, (i - k - 1) % NX] += coef
    one = np.eye(NX)
    full = np.kron(ring, one) + np.kron(one, ring) + 3.0 * CENTER_COEF * np.eye(CELLS)
    return (SCALE * full).astype(np.float32)


def dot32(a, b, dims):
    return lax.dot_general(
        a, b, (dims, ((), ())), precision=lax.Precision.HIGHEST, preferred_element_type=jnp.float32
    )


def filter_kernel(rows, planes, low_hbm, own, pot, high_hbm, mat, out, first, low, high, sem):
    copies = [
        pltpu.make_async_copy(src, dst, sem.at[i])
        for i, (src, dst) in enumerate(((low_hbm, low), (high_hbm, high)))
    ]
    for copy in copies:
        copy.start()

    def field(p):
        if p < planes:
            return low[p * rows : (p + 1) * rows, :]
        if p < 2 * planes:
            return own[(p - planes) * rows : (p - planes + 1) * rows, :]
        return high[(p - 2 * planes) * rows : (p - 2 * planes + 1) * rows, :]

    def level(p):
        if p < planes:
            row = low[planes * rows + p : planes * rows + p + 1, :]
        elif p < 2 * planes:
            row = pot[p - planes : p - planes + 1, :]
        else:
            row = high[planes * rows + p - 2 * planes : planes * rows + p - 2 * planes + 1, :]
        return (row - SHIFT_MID) / HALF_SPAN

    half = RADIUS * rows
    first[half : half + planes * rows, :] = dot32(own[...], mat[...], ((1,), (0,)))
    for copy in copies:
        copy.wait()
    first[0:half, :] = dot32(low[(planes - RADIUS) * rows : planes * rows, :], mat[...], ((1,), (0,)))
    first[half + planes * rows :, :] = dot32(high[0:half, :], mat[...], ((1,), (0,)))
    for q in range(planes + 2 * RADIUS):
        p = q + planes - RADIUS
        acc = first[q * rows : (q + 1) * rows, :] + level(p) * field(p)
        for k in range(RADIUS):
            acc = acc + (SCALE * COEFS[k]) * (field(p + k + 1) + field(p - k - 1))
        first[q * rows : (q + 1) * rows, :] = acc
    inner = dot32(first[half : half + planes * rows, :], mat[...], ((1,), (0,)))
    for z in range(planes):
        q = z + RADIUS
        centre = first[q * rows : (q + 1) * rows, :]
        acc = inner[z * rows : (z + 1) * rows, :] + level(z + planes) * centre
        for k in range(RADIUS):
            up = first[(q + k + 1) * rows : (q + k + 2) * rows, :]
            down = first[(q - k - 1) * rows : (q - k) * rows, :]
            acc = acc + (SCALE * COEFS[k]) * (up + down)
        second = 2.0 * acc - field(z + planes)
        out[2 * z] = second[:, :TILE]
        out[2 * z + 1] = second[:, TILE:]


def gram_kernel(scale, place, own, other, out, stack):
    c = place[0]
    rows = own.shape[2]
    for half, ref in ((c, own), (1 - c, other)):
        for s in range(own.shape[0]):
            for t in range(own.shape[1]):
                at = pl.multiple_of(s * 2 * rows + half * rows, rows)
                stack[pl.ds(at, rows), t * TILE : (t + 1) * TILE] = ref[s, t]
    for k in range(5):
        i = jnp.where(c == 0, BLOCKS[0][k][0], BLOCKS[1][k][0])
        j = jnp.where(c == 0, BLOCKS[0][k][1], BLOCKS[1][k][1])
        a = stack[pl.ds(pl.multiple_of(i * TILE, TILE), TILE), :]
        b = stack[pl.ds(pl.multiple_of(j * TILE, TILE), TILE), :]
        out[k * TILE : (k + 1) * TILE, :] = dot32(a, b, ((1,), (1,))) * scale


def line(block, row):
    return jnp.broadcast_to(block[row : row + 1, :], (8, TILE))


def factor_tile(ref, origin):
    lane = lax.broadcasted_iota(jnp.int32, (8, TILE), 1)
    sub = lax.broadcasted_iota(jnp.int32, (8, TILE), 0)
    lanes = slice(origin, origin + TILE)
    halves = range(GROUP // 8)
    for base in range(0, TILE, GROUP):
        inside = (lane >= base) & (lane < base + GROUP)
        place = [slice(origin + base + 8 * h, origin + base + 8 * h + 8) for h in halves]
        rows = [ref[place[h], lanes] for h in halves]
        col = [
            [jnp.broadcast_to(rows[h][:, base + k : base + k + 1], (8, TILE)) for k in range(GROUP)]
            for h in halves
        ]
        start = [
            jnp.where(inside, jnp.where(lane - base == sub + 8 * h, 1.0, 0.0), rows[h]) for h in halves
        ]
        low, full = list(start), list(start)
        scale = [jnp.zeros((8, TILE), jnp.float32) for _ in halves]
        for j in range(GROUP):
            h, r = divmod(j, 8)
            at = sub == r
            pivot = line(col[h][j], r)
            inv = 1.0 / pivot
            scale[h] = jnp.where(at, lax.rsqrt(pivot), scale[h])
            mine = [col[i][j] for i in halves]
            for k in range(j + 1, GROUP):
                ratio = line(col[h][k], r) * inv
                for i in halves:
                    new = col[i][k] - mine[i] * ratio
                    col[i][k] = jnp.where(at, ratio, new) if i == h else new
            ratio = line(low[h], r) * inv
            for i in range(h, GROUP // 8):
                low[i] = low[i] - (jnp.where(sub > r, mine[i], 0.0) if i == h else mine[i]) * ratio
            ratio = line(full[h], r) * inv
            for i in halves:
                new = full[i] - mine[i] * ratio
                full[i] = jnp.where(at, ratio, new) if i == h else new
        for h in halves:
            ref[place[h], lanes] = jnp.where(lane < base + GROUP, low[h] * scale[h], 0.0)
        for q in range(base + GROUP, TILE, 8):
            rest = ref[origin + q : origin + q + 8, lanes]
            acc = jnp.where(inside, 0.0, rest)
            for m in range(GROUP):
                acc = acc - jnp.broadcast_to(rest[:, base + m : base + m + 1], (8, TILE)) * line(
                    full[m // 8], m % 8
                )
            ref[origin + q : origin + q + 8, lanes] = acc


def factor_kernel(place, own, other, fields, corr, out, work):
    first = place[0] == 0
    for k in range(5):
        rows = slice(k * TILE, (k + 1) * TILE)
        a, b = own[rows, :], other[rows, :]
        for blocks, block in ((BLOCKS[0], jnp.where(first, a, b)), (BLOCKS[1], jnp.where(first, b, a))):
            i, j = blocks[k]
            corr[i * TILE : (i + 1) * TILE, j * TILE : (j + 1) * TILE] = block
            if i != j:
                corr[j * TILE : (j + 1) * TILE, i * TILE : (i + 1) * TILE] = block.T
    work[...] = corr[...]
    count = work.shape[0]
    size = out.shape[2]
    pairs = TILE // (2 * size)
    for k in range(0, count, TILE):
        own_rows = slice(k, k + TILE)
        factor_tile(work, k)
        inverse = work[own_rows, own_rows]
        for side in (slice(0, k), slice(k + TILE, count)):
            if side.start < side.stop:
                work[own_rows, side] = dot32(inverse, work[own_rows, side], ((1,), (0,)))
        mine = [
            work[pl.ds(pl.multiple_of(k + 2 * i * size + place[0] * size, size), size), 0 : k + TILE]
            for i in range(pairs)
        ]
        turned = dot32(jnp.concatenate(mine, axis=0), fields[0 : k + TILE, :], ((1,), (0,)))
        for i in range(pairs):
            for t in range(out.shape[1]):
                out[k // TILE * pairs + i, t] = turned[i * size : (i + 1) * size, t * TILE : (t + 1) * TILE]
        for r in range(k + TILE, count, TILE):
            rows = slice(r, r + TILE)
            lower = work[own_rows, rows].T
            for side in (slice(r, count), slice(0, k)):
                if side.start < side.stop:
                    work[rows, side] = work[rows, side] - dot32(lower, work[own_rows, side], ((1,), (0,)))
            work[rows, own_rows] = -dot32(lower, inverse, ((1,), (0,)))


VMEM = pl.BlockSpec(memory_space=pltpu.VMEM)
ANY = pl.BlockSpec(memory_space=pl.ANY)
SMEM = pl.BlockSpec(memory_space=pltpu.SMEM)
PARAMS = pltpu.CompilerParams(vmem_limit_bytes=48 << 20)


def ring(axes, step):
    count = lax.axis_size(axes)
    return [(i, (i + step) % count) for i in range(count)]


def flip(axes, bits):
    return [(i, i ^ bits) for i in range(lax.axis_size(axes))]


def per_device(orbitals, potential):
    planes, rows, cells = orbitals.shape
    place = lax.axis_index("c").astype(jnp.int32).reshape(1)
    own = orbitals.reshape(planes * rows, cells)
    packed = jnp.concatenate([own, potential], axis=0)
    low = lax.ppermute(packed, SPACE, ring(SPACE, 1))
    high = lax.ppermute(packed, SPACE, ring(SPACE, -1))
    second = pl.pallas_call(
        functools.partial(filter_kernel, rows, planes),
        out_shape=jax.ShapeDtypeStruct((2 * planes, rows, TILE), jnp.float32),
        in_specs=[ANY, VMEM, VMEM, ANY, VMEM],
        out_specs=VMEM,
        scratch_shapes=[
            pltpu.VMEM(((planes + 2 * RADIUS) * rows, cells), jnp.float32),
            pltpu.VMEM(packed.shape, jnp.float32),
            pltpu.VMEM(packed.shape, jnp.float32),
            pltpu.SemaphoreType.DMA((2,)),
        ],
        compiler_params=PARAMS,
        name="filter",
    )(low, own, potential, high, jnp.asarray(plane_matrix()))

    team = lax.axis_size(TEAM)
    mine = lax.all_to_all(second.reshape(team, 2 * planes // team, rows, TILE), TEAM, 0, 0)
    theirs = lax.ppermute(mine, ("c",), flip("c", 1))
    count = 2 * team * rows
    total = float(planes * lax.axis_size(SPACE) * cells)
    part, fields = pl.pallas_call(
        functools.partial(gram_kernel, 1.0 / total),
        out_shape=(
            jax.ShapeDtypeStruct((5 * TILE, TILE), jnp.float32),
            jax.ShapeDtypeStruct((count, mine.shape[1] * TILE), jnp.float32),
        ),
        in_specs=[SMEM, VMEM, VMEM],
        out_specs=(VMEM, VMEM),
        compiler_params=PARAMS,
        name="gram",
    )(place, mine, theirs)

    piece = lax.all_to_all(part.reshape(team, 5 * TILE // team, TILE), TEAM, 0, 0).sum(0)
    for bits in ((1, 2, 3), (4, 8, 12)):
        got = [lax.ppermute(piece, SPACE, flip(SPACE, b)) for b in bits]
        piece = (piece + got[0]) + (got[1] + got[2])
    spread = lax.all_to_all(jnp.broadcast_to(piece, (team,) + piece.shape), TEAM, 0, 0)
    mine_g = spread.reshape(5 * TILE, TILE)
    theirs_g = lax.ppermute(mine_g, ("c",), flip("c", 1))
    correlation, turned = pl.pallas_call(
        factor_kernel,
        out_shape=(
            jax.ShapeDtypeStruct((count, count), jnp.float32),
            jax.ShapeDtypeStruct(mine.shape, jnp.float32),
        ),
        in_specs=[SMEM, VMEM, VMEM, VMEM],
        out_specs=(VMEM, VMEM),
        scratch_shapes=[pltpu.VMEM((count, count), jnp.float32)],
        compiler_params=PARAMS,
        name="factor",
    )(place, mine_g, theirs_g, fields)
    back = lax.all_to_all(turned, TEAM, 0, 0).reshape(planes, 2, rows, TILE)
    return (back.transpose(0, 2, 1, 3).reshape(planes, rows, cells), correlation)


def solution(mesh):
    fine = Mesh(mesh.devices.reshape(8, 2, 4, 2, 2), ("z", "xh", "y", "xl", "c"))
    return jax.shard_map(
        per_device,
        mesh=fine,
        in_specs=(P(SPACE, BAND, None), P(SPACE, None)),
        out_specs=(P(SPACE, BAND, None), P()),
        check_vma=False,
    )
```

```python
import functools

import jax
import jax.numpy as jnp
import numpy as np
from jax import lax
from jax.experimental import pallas as pl
from jax.experimental.pallas import tpu as pltpu
from jax.sharding import Mesh
from jax.sharding import PartitionSpec as P

NX = 16
NY = 16
CELLS = NX * NY
COEFS = [12.0 / 7.0, -15.0 / 56.0, 10.0 / 189.0, -1.0 / 112.0, 2.0 / 1925.0, -1.0 / 16632.0]
CENTER_COEF = -5369.0 / 1800.0
INV_SPACING2 = 6.25
SHIFT_MID = 42.0
HALF_SPAN = 38.0
RADIUS = 6

SPACE = ("z", "xh")
TEAM = ("y", "xl")
LAYER = ("xh", "y", "xl")
BAND = ("y", "xl", "c")

BLOCKS = [[(0, 0), (1, 0), (1, 1), (2, 0), (2, 1)], [(2, 2), (3, 0), (3, 1), (3, 2), (3, 3)]]
TILE = 128
GROUP = 16

SCALE = -0.5 * INV_SPACING2 / HALF_SPAN


def plane_matrix():
    ring = np.zeros((NX, NX))
    for k, coef in enumerate(COEFS):
        for i in range(NX):
            ring[i, (i + k + 1) % NX] += coef
            ring[i, (i - k - 1) % NX] += coef
    one = np.eye(NX)
    full = np.kron(ring, one) + np.kron(one, ring) + 3.0 * CENTER_COEF * np.eye(CELLS)
    return (SCALE * full).astype(np.float32)


def dot32(a, b, dims):
    return lax.dot_general(
        a, b, (dims, ((), ())), precision=lax.Precision.HIGHEST, preferred_element_type=jnp.float32
    )


def level(pot, p):
    return (pot[p : p + 1, :] - SHIFT_MID) / HALF_SPAN


def begin_kernel(rows, planes, own, pot, mat, out):
    flat = dot32(own[...], mat[...], ((1,), (0,)))
    for z in range(planes):
        acc = flat[z * rows : (z + 1) * rows, :] + level(pot, z) * own[z * rows : (z + 1) * rows, :]
        for k in range(RADIUS):
            near = [own[p * rows : (p + 1) * rows, :] for p in (z + k + 1, z - k - 1) if 0 <= p < planes]
            acc = acc + (SCALE * COEFS[k]) * sum(near[1:], near[0])
        out[z * rows : (z + 1) * rows, :] = acc


def filter_kernel(rows, planes, low, own, high, pot_low, pot, pot_high, mat, part, out, first):
    def field(p):
        ref = (low, own, high)[p // planes]
        return ref[p % planes * rows : (p % planes + 1) * rows, :]

    def missing(acc, p, known):
        for k in range(RADIUS):
            far = [field(q) for q in (p + k + 1, p - k - 1) if not (known and planes <= q < 2 * planes)]
            if far:
                acc = acc + (SCALE * COEFS[k]) * sum(far[1:], far[0])
        return acc

    half = RADIUS * rows
    size = planes * rows
    first[0:half, :] = dot32(low[size - half : size, :], mat[...], ((1,), (0,)))
    first[half + size :, :] = dot32(high[0:half, :], mat[...], ((1,), (0,)))
    for q in range(planes + 2 * RADIUS):
        p = q + planes - RADIUS
        at = slice(q * rows, (q + 1) * rows)
        if planes <= p < 2 * planes:
            first[at, :] = missing(part[(p - planes) * rows : (p - planes + 1) * rows, :], p, True)
        else:
            row = level((pot_low, pot, pot_high)[p // planes], p % planes)
            first[at, :] = missing(first[at, :] + row * field(p), p, False)
    inner = dot32(first[half : half + size, :], mat[...], ((1,), (0,)))
    for z in range(planes):
        q = z + RADIUS
        centre = first[q * rows : (q + 1) * rows, :]
        acc = inner[z * rows : (z + 1) * rows, :] + level(pot, z) * centre
        for k in range(RADIUS):
            up = first[(q + k + 1) * rows : (q + k + 2) * rows, :]
            down = first[(q - k - 1) * rows : (q - k) * rows, :]
            acc = acc + (SCALE * COEFS[k]) * (up + down)
        second = 2.0 * acc - field(z + planes)
        out[2 * z] = second[:, :TILE]
        out[2 * z + 1] = second[:, TILE:]


def gram_kernel(scale, place, own, other, out, stack):
    c = place[0]
    rows = own.shape[2]
    for half, ref in ((c, own), (1 - c, other)):
        for s in range(own.shape[0]):
            for t in range(own.shape[1]):
                at = pl.multiple_of(s * 2 * rows + half * rows, rows)
                stack[pl.ds(at, rows), t * TILE : (t + 1) * TILE] = ref[s, t]
    for k in range(5):
        i = jnp.where(c == 0, BLOCKS[0][k][0], BLOCKS[1][k][0])
        j = jnp.where(c == 0, BLOCKS[0][k][1], BLOCKS[1][k][1])
        a = stack[pl.ds(pl.multiple_of(i * TILE, TILE), TILE), :]
        b = stack[pl.ds(pl.multiple_of(j * TILE, TILE), TILE), :]
        out[k * TILE : (k + 1) * TILE, :] = dot32(a, b, ((1,), (1,))) * scale


def line(block, row):
    return jnp.broadcast_to(block[row : row + 1, :], (8, TILE))


def factor_tile(ref, origin):
    lane = lax.broadcasted_iota(jnp.int32, (8, TILE), 1)
    sub = lax.broadcasted_iota(jnp.int32, (8, TILE), 0)
    lanes = slice(origin, origin + TILE)
    halves = range(GROUP // 8)
    for base in range(0, TILE, GROUP):
        inside = (lane >= base) & (lane < base + GROUP)
        place = [slice(origin + base + 8 * h, origin + base + 8 * h + 8) for h in halves]
        rows = [ref[place[h], lanes] for h in halves]
        col = [
            [jnp.broadcast_to(rows[h][:, base + k : base + k + 1], (8, TILE)) for k in range(GROUP)]
            for h in halves
        ]
        start = [
            jnp.where(inside, jnp.where(lane - base == sub + 8 * h, 1.0, 0.0), rows[h]) for h in halves
        ]
        low, full = list(start), list(start)
        scale = [jnp.zeros((8, TILE), jnp.float32) for _ in halves]
        for j in range(GROUP):
            h, r = divmod(j, 8)
            at = sub == r
            pivot = line(col[h][j], r)
            inv = 1.0 / pivot
            scale[h] = jnp.where(at, lax.rsqrt(pivot), scale[h])
            mine = [col[i][j] for i in halves]
            for k in range(j + 1, GROUP):
                ratio = line(col[h][k], r) * inv
                for i in halves:
                    new = col[i][k] - mine[i] * ratio
                    col[i][k] = jnp.where(at, ratio, new) if i == h else new
            ratio = line(low[h], r) * inv
            for i in range(h, GROUP // 8):
                low[i] = low[i] - (jnp.where(sub > r, mine[i], 0.0) if i == h else mine[i]) * ratio
            ratio = line(full[h], r) * inv
            for i in halves:
                new = full[i] - mine[i] * ratio
                full[i] = jnp.where(at, ratio, new) if i == h else new
        for h in halves:
            ref[place[h], lanes] = jnp.where(lane < base + GROUP, low[h] * scale[h], 0.0)
        for q in range(base + GROUP, min(base + 2 * GROUP, TILE), 8):
            rest = ref[origin + q : origin + q + 8, lanes]
            acc = jnp.where(inside, 0.0, rest)
            for m in range(GROUP):
                acc = acc - jnp.broadcast_to(rest[:, base + m : base + m + 1], (8, TILE)) * line(
                    full[m // 8], m % 8
                )
            ref[origin + q : origin + q + 8, lanes] = acc
        if base + 2 * GROUP < TILE:
            far = slice(origin + base + 2 * GROUP, origin + TILE)
            rest = ref[far, lanes]
            column = lax.broadcasted_iota(jnp.int32, rest.shape, 1)
            among = (column >= base) & (column < base + GROUP)
            after = jnp.zeros((TILE - GROUP - base, TILE), jnp.float32)
            before = [jnp.zeros((base, TILE), jnp.float32)] if base else []
            spread = jnp.concatenate(before + full + [after], axis=0)
            ref[far, lanes] = jnp.where(among, 0.0, rest) - dot32(
                jnp.where(among, rest, 0.0), spread, ((1,), (0,))
            )


def factor_kernel(place, own, other, fields, corr, out, work):
    first = place[0] == 0
    for k in range(5):
        rows = slice(k * TILE, (k + 1) * TILE)
        a, b = own[rows, :], other[rows, :]
        for blocks, block in ((BLOCKS[0], jnp.where(first, a, b)), (BLOCKS[1], jnp.where(first, b, a))):
            i, j = blocks[k]
            corr[i * TILE : (i + 1) * TILE, j * TILE : (j + 1) * TILE] = block
            if i != j:
                corr[j * TILE : (j + 1) * TILE, i * TILE : (i + 1) * TILE] = block.T
    work[...] = corr[...]
    count = work.shape[0]
    size = out.shape[2]
    pairs = TILE // (2 * size)
    for k in range(0, count, TILE):
        own_rows = slice(k, k + TILE)
        factor_tile(work, k)
        inverse = work[own_rows, own_rows]
        for side in (slice(0, k), slice(k + TILE, count)):
            if side.start < side.stop:
                work[own_rows, side] = dot32(inverse, work[own_rows, side], ((1,), (0,)))
        mine = [
            work[pl.ds(pl.multiple_of(k + 2 * i * size + place[0] * size, size), size), 0 : k + TILE]
            for i in range(pairs)
        ]
        turned = dot32(jnp.concatenate(mine, axis=0), fields[0 : k + TILE, :], ((1,), (0,)))
        for i in range(pairs):
            for t in range(out.shape[1]):
                out[k // TILE * pairs + i, t] = turned[i * size : (i + 1) * size, t * TILE : (t + 1) * TILE]
        for r in range(k + TILE, count, TILE):
            rows = slice(r, r + TILE)
            lower = work[own_rows, rows].T
            for side in (slice(r, count), slice(0, k)):
                if side.start < side.stop:
                    work[rows, side] = work[rows, side] - dot32(lower, work[own_rows, side], ((1,), (0,)))
            work[rows, own_rows] = -dot32(lower, inverse, ((1,), (0,)))


VMEM = pl.BlockSpec(memory_space=pltpu.VMEM)
SMEM = pl.BlockSpec(memory_space=pltpu.SMEM)
PARAMS = pltpu.CompilerParams(vmem_limit_bytes=48 << 20)


def ring(axes, step):
    count = lax.axis_size(axes)
    return [(i, (i + step) % count) for i in range(count)]


def flip(axes, bits):
    return [(i, i ^ bits) for i in range(lax.axis_size(axes))]


def per_device(orbitals, potential):
    planes, rows, cells = orbitals.shape
    place = lax.axis_index("c").astype(jnp.int32).reshape(1)
    own = orbitals.reshape(planes * rows, cells)
    low = lax.ppermute(own, SPACE, ring(SPACE, 1))
    high = lax.ppermute(own, SPACE, ring(SPACE, -1))
    pot_low = lax.ppermute(potential, SPACE, ring(SPACE, 1))
    pot_high = lax.ppermute(potential, SPACE, ring(SPACE, -1))
    mat = jnp.asarray(plane_matrix())
    begun = pl.pallas_call(
        functools.partial(begin_kernel, rows, planes),
        out_shape=jax.ShapeDtypeStruct(own.shape, jnp.float32),
        in_specs=[VMEM] * 3,
        out_specs=VMEM,
        compiler_params=PARAMS,
        name="begin",
    )(own, potential, mat)
    second = pl.pallas_call(
        functools.partial(filter_kernel, rows, planes),
        out_shape=jax.ShapeDtypeStruct((2 * planes, rows, TILE), jnp.float32),
        in_specs=[VMEM] * 8,
        out_specs=VMEM,
        scratch_shapes=[pltpu.VMEM(((planes + 2 * RADIUS) * rows, cells), jnp.float32)],
        compiler_params=PARAMS,
        name="filter",
    )(low, own, high, pot_low, potential, pot_high, mat, begun)

    team = lax.axis_size(TEAM)
    mine = lax.all_to_all(second.reshape(team, 2 * planes // team, rows, TILE), TEAM, 0, 0)
    theirs = lax.ppermute(mine, ("c",), flip("c", 1))
    count = 2 * team * rows
    total = float(planes * lax.axis_size(SPACE) * cells)
    part, fields = pl.pallas_call(
        functools.partial(gram_kernel, 1.0 / total),
        out_shape=(
            jax.ShapeDtypeStruct((5 * TILE, TILE), jnp.float32),
            jax.ShapeDtypeStruct((count, mine.shape[1] * TILE), jnp.float32),
        ),
        in_specs=[SMEM, VMEM, VMEM],
        out_specs=(VMEM, VMEM),
        compiler_params=PARAMS,
        name="gram",
    )(place, mine, theirs)

    layer = lax.axis_size(LAYER)
    piece = lax.all_to_all(part.reshape(layer, 5 * TILE // layer, TILE), LAYER, 0, 0).sum(0)
    piece = piece + lax.ppermute(piece, "z", flip("z", 1))
    got = [lax.ppermute(piece, "z", flip("z", b)) for b in (2, 4, 6)]
    piece = (piece + got[0]) + (got[1] + got[2])
    spread = lax.all_to_all(jnp.broadcast_to(piece, (layer,) + piece.shape), LAYER, 0, 0)
    mine_g = spread.reshape(5 * TILE, TILE)
    theirs_g = lax.ppermute(mine_g, ("c",), flip("c", 1))
    correlation, turned = pl.pallas_call(
        factor_kernel,
        out_shape=(
            jax.ShapeDtypeStruct((count, count), jnp.float32),
            jax.ShapeDtypeStruct(mine.shape, jnp.float32),
        ),
        in_specs=[SMEM, VMEM, VMEM, VMEM],
        out_specs=(VMEM, VMEM),
        scratch_shapes=[pltpu.VMEM((count, count), jnp.float32)],
        compiler_params=PARAMS,
        name="factor",
    )(place, mine_g, theirs_g, fields)
    back = lax.all_to_all(turned, TEAM, 0, 0).reshape(planes, 2, rows, TILE)
    return (back.transpose(0, 2, 1, 3).reshape(planes, rows, cells), correlation)


def solution(mesh):
    fine = Mesh(mesh.devices.reshape(8, 2, 4, 2, 2), ("z", "xh", "y", "xl", "c"))
    return jax.shard_map(
        per_device,
        mesh=fine,
        in_specs=(P(SPACE, BAND, None), P(SPACE, None)),
        out_specs=(P(SPACE, BAND, None), P()),
        check_vma=False,
    )
```

```python
import functools

import jax
import jax.numpy as jnp
import numpy as np
from jax import lax
from jax.experimental import pallas as pl
from jax.experimental.pallas import tpu as pltpu
from jax.sharding import Mesh
from jax.sharding import PartitionSpec as P

NX = 16
NY = 16
CELLS = NX * NY
COEFS = [12.0 / 7.0, -15.0 / 56.0, 10.0 / 189.0, -1.0 / 112.0, 2.0 / 1925.0, -1.0 / 16632.0]
CENTER_COEF = -5369.0 / 1800.0
INV_SPACING2 = 6.25
SHIFT_MID = 42.0
HALF_SPAN = 38.0
RADIUS = 6

SPACE = ("z", "xh")
TEAM = ("y", "xl")
LAYER = ("xh", "y", "xl")
BAND = ("y", "xl", "c")

BLOCKS = [[(0, 0), (1, 0), (1, 1), (2, 0), (2, 1)], [(2, 2), (3, 0), (3, 1), (3, 2), (3, 3)]]
TILE = 128
GROUP = 16

SCALE = -0.5 * INV_SPACING2 / HALF_SPAN


def plane_matrix():
    ring = np.zeros((NX, NX))
    for k, coef in enumerate(COEFS):
        for i in range(NX):
            ring[i, (i + k + 1) % NX] += coef
            ring[i, (i - k - 1) % NX] += coef
    one = np.eye(NX)
    full = np.kron(ring, one) + np.kron(one, ring) + 3.0 * CENTER_COEF * np.eye(CELLS)
    return (SCALE * full).astype(np.float32)


def dot32(a, b, dims):
    return lax.dot_general(
        a, b, (dims, ((), ())), precision=lax.Precision.HIGHEST, preferred_element_type=jnp.float32
    )


def filter_kernel(
    rows, planes, place, own, swap, near, cross, pot, pot_swap, pot_near, pot_cross, mat, out, field, level, first
):
    h = place[1]
    size = planes * rows
    for k, data, values in (
        (1 + h, own, pot),
        (2 - h, swap, pot_swap),
        (3 - 3 * h, near, pot_near),
        (3 * h, cross, pot_cross),
    ):
        field[pl.ds(pl.multiple_of(k * size, size), size), :] = data[...]
        level[k, 0:planes, :] = (values[...] - SHIFT_MID) / HALF_SPAN

    def plane(ref, p):
        return ref[p * rows : (p + 1) * rows, :]

    def row(p):
        return level[p // planes, p % planes : p % planes + 1, :]

    skip = planes - RADIUS
    count = 2 * planes + 2 * RADIUS
    first[...] = dot32(field[skip * rows : (skip + count) * rows, :], mat[...], ((1,), (0,)))
    for q in range(count):
        p = q + skip
        acc = plane(first, q) + row(p) * plane(field, p)
        for k in range(RADIUS):
            acc = acc + (SCALE * COEFS[k]) * (plane(field, p + k + 1) + plane(field, p - k - 1))
        first[q * rows : (q + 1) * rows, :] = acc
    inner = dot32(first[RADIUS * rows : RADIUS * rows + 2 * size, :], mat[...], ((1,), (0,)))
    for z in range(2 * planes):
        q = z + RADIUS
        acc = inner[z * rows : (z + 1) * rows, :] + row(z + planes) * plane(first, q)
        for k in range(RADIUS):
            acc = acc + (SCALE * COEFS[k]) * (plane(first, q + k + 1) + plane(first, q - k - 1))
        second = 2.0 * acc - plane(field, z + planes)
        out[2 * z] = second[:, :TILE]
        out[2 * z + 1] = second[:, TILE:]


def gram_kernel(scale, place, own, other, out, stack):
    c = place[0]
    rows = own.shape[2]
    team = own.shape[0] // 2
    for half, ref in ((c, own), (1 - c, other)):
        for s in range(own.shape[0]):
            at = pl.multiple_of((s % team * 4 + half * 2 + s // team) * rows, rows)
            for t in range(own.shape[1]):
                stack[pl.ds(at, rows), t * TILE : (t + 1) * TILE] = ref[s, t]
    for k in range(5):
        i = jnp.where(c == 0, BLOCKS[0][k][0], BLOCKS[1][k][0])
        j = jnp.where(c == 0, BLOCKS[0][k][1], BLOCKS[1][k][1])
        a = stack[pl.ds(pl.multiple_of(i * TILE, TILE), TILE), :]
        b = stack[pl.ds(pl.multiple_of(j * TILE, TILE), TILE), :]
        out[k * TILE : (k + 1) * TILE, :] = dot32(a, b, ((1,), (1,))) * scale


def line(block, row):
    return jnp.broadcast_to(block[row : row + 1, :], (8, TILE))


def factor_tile(ref, origin):
    lane = lax.broadcasted_iota(jnp.int32, (8, TILE), 1)
    sub = lax.broadcasted_iota(jnp.int32, (8, TILE), 0)
    lanes = slice(origin, origin + TILE)
    halves = range(GROUP // 8)
    for base in range(0, TILE, GROUP):
        inside = (lane >= base) & (lane < base + GROUP)
        place = [slice(origin + base + 8 * h, origin + base + 8 * h + 8) for h in halves]
        rows = [ref[place[h], lanes] for h in halves]
        col = [
            [jnp.broadcast_to(rows[h][:, base + k : base + k + 1], (8, TILE)) for k in range(GROUP)]
            for h in halves
        ]
        start = [
            jnp.where(inside, jnp.where(lane - base == sub + 8 * h, 1.0, 0.0), rows[h]) for h in halves
        ]
        low, full = list(start), list(start)
        scale = [jnp.zeros((8, TILE), jnp.float32) for _ in halves]
        for j in range(GROUP):
            h, r = divmod(j, 8)
            at = sub == r
            pivot = line(col[h][j], r)
            inv = 1.0 / pivot
            scale[h] = jnp.where(at, lax.rsqrt(pivot), scale[h])
            mine = [col[i][j] for i in halves]
            for k in range(j + 1, GROUP):
                ratio = line(col[h][k], r) * inv
                for i in halves:
                    new = col[i][k] - mine[i] * ratio
                    col[i][k] = jnp.where(at, ratio, new) if i == h else new
            ratio = line(low[h], r) * inv
            for i in range(h, GROUP // 8):
                low[i] = low[i] - (jnp.where(sub > r, mine[i], 0.0) if i == h else mine[i]) * ratio
            ratio = line(full[h], r) * inv
            for i in halves:
                new = full[i] - mine[i] * ratio
                full[i] = jnp.where(at, ratio, new) if i == h else new
        for h in halves:
            ref[place[h], lanes] = jnp.where(lane < base + GROUP, low[h] * scale[h], 0.0)
        for q in range(base + GROUP, min(base + 2 * GROUP, TILE), 8):
            rest = ref[origin + q : origin + q + 8, lanes]
            acc = jnp.where(inside, 0.0, rest)
            for m in range(GROUP):
                acc = acc - jnp.broadcast_to(rest[:, base + m : base + m + 1], (8, TILE)) * line(
                    full[m // 8], m % 8
                )
            ref[origin + q : origin + q + 8, lanes] = acc
        if base + 2 * GROUP < TILE:
            far = slice(origin + base + 2 * GROUP, origin + TILE)
            rest = ref[far, lanes]
            column = lax.broadcasted_iota(jnp.int32, rest.shape, 1)
            among = (column >= base) & (column < base + GROUP)
            after = jnp.zeros((TILE - GROUP - base, TILE), jnp.float32)
            before = [jnp.zeros((base, TILE), jnp.float32)] if base else []
            spread = jnp.concatenate(before + full + [after], axis=0)
            ref[far, lanes] = jnp.where(among, 0.0, rest) - dot32(
                jnp.where(among, rest, 0.0), spread, ((1,), (0,))
            )


def factor_kernel(place, own, other, fields, corr, out, work):
    first = place[0] == 0
    for k in range(5):
        rows = slice(k * TILE, (k + 1) * TILE)
        a, b = own[rows, :], other[rows, :]
        for blocks, block in ((BLOCKS[0], jnp.where(first, a, b)), (BLOCKS[1], jnp.where(first, b, a))):
            i, j = blocks[k]
            corr[i * TILE : (i + 1) * TILE, j * TILE : (j + 1) * TILE] = block
            if i != j:
                corr[j * TILE : (j + 1) * TILE, i * TILE : (i + 1) * TILE] = block.T
    work[...] = corr[...]
    count = work.shape[0]
    size = out.shape[2]
    pairs = TILE // (2 * size)
    for k in range(0, count, TILE):
        own_rows = slice(k, k + TILE)
        factor_tile(work, k)
        inverse = work[own_rows, own_rows]
        for side in (slice(0, k), slice(k + TILE, count)):
            if side.start < side.stop:
                work[own_rows, side] = dot32(inverse, work[own_rows, side], ((1,), (0,)))
        mine = [
            work[pl.ds(pl.multiple_of(k + 2 * i * size + place[0] * size, size), size), 0 : k + TILE]
            for i in range(pairs)
        ]
        turned = dot32(jnp.concatenate(mine, axis=0), fields[0 : k + TILE, :], ((1,), (0,)))
        for i in range(pairs):
            for t in range(out.shape[1]):
                out[k // TILE * pairs + i, t] = turned[i * size : (i + 1) * size, t * TILE : (t + 1) * TILE]
        for r in range(k + TILE, count, TILE):
            rows = slice(r, r + TILE)
            lower = work[own_rows, rows].T
            for side in (slice(r, count), slice(0, k)):
                if side.start < side.stop:
                    work[rows, side] = work[rows, side] - dot32(lower, work[own_rows, side], ((1,), (0,)))
            work[rows, own_rows] = -dot32(lower, inverse, ((1,), (0,)))


VMEM = pl.BlockSpec(memory_space=pltpu.VMEM)
SMEM = pl.BlockSpec(memory_space=pltpu.SMEM)
PARAMS = pltpu.CompilerParams(vmem_limit_bytes=48 << 20)


def flip(axes, bits):
    return [(i, i ^ bits) for i in range(lax.axis_size(axes))]


def per_device(orbitals, potential):
    planes, rows, cells = orbitals.shape
    side = lax.axis_index("xh")
    place = jnp.stack([lax.axis_index("c"), side]).astype(jnp.int32)
    half = rows // 2
    own, other = (
        lax.dynamic_slice_in_dim(orbitals, at * half, half, 1).reshape(planes * half, cells)
        for at in (side, 1 - side)
    )
    slabs = lax.axis_size(SPACE)
    swap = [(s, s ^ 1) for s in range(slabs)]
    near = [(s, (s + 2 * (2 * (s % 2) - 1)) % slabs) for s in range(slabs)]
    cross = [(s, (s + 2 * (s % 2) - 1) % slabs) for s in range(slabs)]
    data = [lax.ppermute(x, SPACE, pairs) for x, pairs in ((other, cross), (other, swap), (own, near))][::-1]
    pots = [lax.ppermute(potential, SPACE, pairs) for pairs in (cross, swap, near)][::-1]
    near, swap, cross = data
    pot_near, pot_swap, pot_cross = pots
    second = pl.pallas_call(
        functools.partial(filter_kernel, half, planes),
        out_shape=jax.ShapeDtypeStruct((4 * planes, half, TILE), jnp.float32),
        in_specs=[SMEM] + [VMEM] * 9,
        out_specs=VMEM,
        scratch_shapes=[
            pltpu.VMEM((4 * planes * half, cells), jnp.float32),
            pltpu.VMEM((4, 16, cells), jnp.float32),
            pltpu.VMEM(((2 * planes + 2 * RADIUS) * half, cells), jnp.float32),
        ],
        compiler_params=PARAMS,
        name="filter",
    )(place, own, swap, near, cross, potential, pot_swap, pot_near, pot_cross, jnp.asarray(plane_matrix()))

    team, layer = lax.axis_size(TEAM), lax.axis_size(LAYER)
    mine = lax.all_to_all(second.reshape(layer, 4 * planes // layer, half, TILE), LAYER, 0, 0)
    theirs = lax.ppermute(mine, ("c",), flip("c", 1))
    count = 2 * team * rows
    total = float(planes * lax.axis_size(SPACE) * cells)
    part, fields = pl.pallas_call(
        functools.partial(gram_kernel, 1.0 / total),
        out_shape=(
            jax.ShapeDtypeStruct((5 * TILE, TILE), jnp.float32),
            jax.ShapeDtypeStruct((count, mine.shape[1] * TILE), jnp.float32),
        ),
        in_specs=[SMEM, VMEM, VMEM],
        out_specs=(VMEM, VMEM),
        compiler_params=PARAMS,
        name="gram",
    )(place, mine, theirs)

    piece = lax.all_to_all(part.reshape(layer, 5 * TILE // layer, TILE), LAYER, 0, 0).sum(0)
    piece = piece + lax.ppermute(piece, "z", flip("z", 1))
    got = [lax.ppermute(piece, "z", flip("z", b)) for b in (2, 4, 6)]
    piece = (piece + got[0]) + (got[1] + got[2])
    spread = lax.all_to_all(jnp.broadcast_to(piece, (layer,) + piece.shape), LAYER, 0, 0)
    mine_g = spread.reshape(5 * TILE, TILE)
    theirs_g = lax.ppermute(mine_g, ("c",), flip("c", 1))
    correlation, turned = pl.pallas_call(
        factor_kernel,
        out_shape=(
            jax.ShapeDtypeStruct((count, count), jnp.float32),
            jax.ShapeDtypeStruct((team, mine.shape[1], rows, TILE), jnp.float32),
        ),
        in_specs=[SMEM, VMEM, VMEM, VMEM],
        out_specs=(VMEM, VMEM),
        scratch_shapes=[pltpu.VMEM((count, count), jnp.float32)],
        compiler_params=PARAMS,
        name="factor",
    )(place, mine_g, theirs_g, fields)
    back = lax.all_to_all(turned, TEAM, 0, 0).reshape(planes, 2, rows, TILE)
    return (back.transpose(0, 2, 1, 3).reshape(planes, rows, cells), correlation)


def solution(mesh):
    fine = Mesh(mesh.devices.reshape(8, 2, 4, 2, 2), ("z", "xh", "y", "xl", "c"))
    return jax.shard_map(
        per_device,
        mesh=fine,
        in_specs=(P(SPACE, BAND, None), P(SPACE, None)),
        out_specs=(P(SPACE, BAND, None), P()),
        check_vma=False,
    )
```

```python
import functools

import jax
import jax.numpy as jnp
import numpy as np
from jax import lax
from jax.experimental import pallas as pl
from jax.experimental.pallas import tpu as pltpu
from jax.sharding import Mesh
from jax.sharding import PartitionSpec as P

NX = 16
NY = 16
CELLS = NX * NY
COEFS = [12.0 / 7.0, -15.0 / 56.0, 10.0 / 189.0, -1.0 / 112.0, 2.0 / 1925.0, -1.0 / 16632.0]
CENTER_COEF = -5369.0 / 1800.0
INV_SPACING2 = 6.25
SHIFT_MID = 42.0
HALF_SPAN = 38.0
RADIUS = 6

SPACE = ("z", "xh")
TEAM = ("y", "xl")
LAYER = ("xh", "y", "xl")
BAND = ("y", "xl", "c")

BLOCKS = [[(0, 0), (1, 0), (1, 1), (2, 0), (2, 1)], [(2, 2), (3, 0), (3, 1), (3, 2), (3, 3)]]
TILE = 128
GROUP = 16

SCALE = -0.5 * INV_SPACING2 / HALF_SPAN


def plane_matrix():
    ring = np.zeros((NX, NX))
    for k, coef in enumerate(COEFS):
        for i in range(NX):
            ring[i, (i + k + 1) % NX] += coef
            ring[i, (i - k - 1) % NX] += coef
    one = np.eye(NX)
    full = np.kron(ring, one) + np.kron(one, ring) + 3.0 * CENTER_COEF * np.eye(CELLS)
    return (SCALE * full).astype(np.float32)


def dot32(a, b, dims):
    return lax.dot_general(
        a, b, (dims, ((), ())), precision=lax.Precision.HIGHEST, preferred_element_type=jnp.float32
    )


def filter_kernel(rows, planes, side, own, swap, near, cross, mat, out, first):
    size = planes * rows
    count = 2 * planes + 2 * RADIUS

    def filter_slabs(slabs):
        def field(p):
            return slabs[p // planes][p % planes * rows : (p % planes + 1) * rows, :]

        def level(p):
            at = size + p % planes
            return (slabs[p // planes][at : at + 1, :] - SHIFT_MID) / HALF_SPAN

        def plane(q):
            return first[q * rows : (q + 1) * rows, :]

        skip = planes - RADIUS
        for k, slab in enumerate(slabs):
            begin, end = max(k * planes, skip), min((k + 1) * planes, skip + count)
            part = slab[(begin - k * planes) * rows : (end - k * planes) * rows, :]
            first[(begin - skip) * rows : (end - skip) * rows, :] = dot32(part, mat[...], ((1,), (0,)))
        for q in range(count):
            p = q + skip
            acc = plane(q) + level(p) * field(p)
            for k in range(RADIUS):
                acc = acc + (SCALE * COEFS[k]) * (field(p + k + 1) + field(p - k - 1))
            first[q * rows : (q + 1) * rows, :] = acc
        inner = dot32(first[RADIUS * rows : RADIUS * rows + 2 * size, :], mat[...], ((1,), (0,)))
        for z in range(2 * planes):
            q = z + RADIUS
            acc = inner[z * rows : (z + 1) * rows, :] + level(z + planes) * plane(q)
            for k in range(RADIUS):
                acc = acc + (SCALE * COEFS[k]) * (plane(q + k + 1) + plane(q - k - 1))
            second = 2.0 * acc - field(z + planes)
            out[2 * z] = second[:, :TILE]
            out[2 * z + 1] = second[:, TILE:]

    @pl.when(side[0] == 0)
    def _():
        filter_slabs((cross, own, swap, near))

    @pl.when(side[0] == 1)
    def _():
        filter_slabs((near, swap, own, cross))


def gram_kernel(scale, core, own, other, out, stack):
    rows = own.shape[2]
    team = own.shape[0] // 2

    def gram_tiles(c):
        for half, ref in ((c, own), (1 - c, other)):
            for s in range(own.shape[0]):
                at = (s % team * 4 + half * 2 + s // team) * rows
                for t in range(own.shape[1]):
                    stack[at : at + rows, t * TILE : (t + 1) * TILE] = ref[s, t]
        for k, wide in ((0, 1), (1, 2), (3, 2)):
            i, j = BLOCKS[c][k]
            tiles = scale * dot32(
                stack[i * TILE : (i + 1) * TILE, :], stack[j * TILE : (j + wide) * TILE, :], ((1,), (1,))
            )
            for w in range(wide):
                out[(k + w) * TILE : (k + w + 1) * TILE, :] = tiles[:, w * TILE : (w + 1) * TILE]

    @pl.when(core[0] == 0)
    def _():
        gram_tiles(0)

    @pl.when(core[0] == 1)
    def _():
        gram_tiles(1)


def line(block, row):
    return jnp.broadcast_to(block[row : row + 1, :], (8, TILE))


def factor_tile(ref, origin):
    lane = lax.broadcasted_iota(jnp.int32, (8, TILE), 1)
    sub = lax.broadcasted_iota(jnp.int32, (8, TILE), 0)
    lanes = slice(origin, origin + TILE)
    halves = range(GROUP // 8)
    for base in range(0, TILE, GROUP):
        inside = (lane >= base) & (lane < base + GROUP)
        place = [slice(origin + base + 8 * h, origin + base + 8 * h + 8) for h in halves]
        rows = [ref[place[h], lanes] for h in halves]
        col = [
            [jnp.broadcast_to(rows[h][:, base + k : base + k + 1], (8, TILE)) for k in range(GROUP)]
            for h in halves
        ]
        start = [
            jnp.where(inside, jnp.where(lane - base == sub + 8 * h, 1.0, 0.0), rows[h]) for h in halves
        ]
        low, full = list(start), list(start)
        scale = [jnp.zeros((8, TILE), jnp.float32) for _ in halves]
        for j in range(GROUP):
            h, r = divmod(j, 8)
            at = sub == r
            pivot = line(col[h][j], r)
            inv = 1.0 / pivot
            scale[h] = jnp.where(at, lax.rsqrt(pivot), scale[h])
            mine = [col[i][j] for i in halves]
            for k in range(j + 1, GROUP):
                ratio = line(col[h][k], r) * inv
                for i in halves:
                    new = col[i][k] - mine[i] * ratio
                    col[i][k] = jnp.where(at, ratio, new) if i == h else new
            ratio = line(low[h], r) * inv
            for i in range(h, GROUP // 8):
                low[i] = low[i] - (jnp.where(sub > r, mine[i], 0.0) if i == h else mine[i]) * ratio
            ratio = line(full[h], r) * inv
            for i in halves:
                new = full[i] - mine[i] * ratio
                full[i] = jnp.where(at, ratio, new) if i == h else new
        for h in halves:
            ref[place[h], lanes] = jnp.where(lane < base + GROUP, low[h] * scale[h], 0.0)
        for q in range(base + GROUP, min(base + 2 * GROUP, TILE), 8):
            rest = ref[origin + q : origin + q + 8, lanes]
            acc = jnp.where(inside, 0.0, rest)
            for m in range(GROUP):
                acc = acc - jnp.broadcast_to(rest[:, base + m : base + m + 1], (8, TILE)) * line(
                    full[m // 8], m % 8
                )
            ref[origin + q : origin + q + 8, lanes] = acc
        if base + 2 * GROUP < TILE:
            far = slice(origin + base + 2 * GROUP, origin + TILE)
            rest = ref[far, lanes]
            column = lax.broadcasted_iota(jnp.int32, rest.shape, 1)
            among = (column >= base) & (column < base + GROUP)
            after = jnp.zeros((TILE - GROUP - base, TILE), jnp.float32)
            before = [jnp.zeros((base, TILE), jnp.float32)] if base else []
            spread = jnp.concatenate(before + full + [after], axis=0)
            ref[far, lanes] = jnp.where(among, 0.0, rest) - dot32(
                jnp.where(among, rest, 0.0), spread, ((1,), (0,))
            )


def factor_kernel(core, own, other, fields, corr, out, work):
    first = core[0] == 0
    for k in range(5):
        rows = slice(k * TILE, (k + 1) * TILE)
        a, b = own[rows, :], other[rows, :]
        for blocks, block in ((BLOCKS[0], jnp.where(first, a, b)), (BLOCKS[1], jnp.where(first, b, a))):
            i, j = blocks[k]
            corr[i * TILE : (i + 1) * TILE, j * TILE : (j + 1) * TILE] = block
            if i != j:
                corr[j * TILE : (j + 1) * TILE, i * TILE : (i + 1) * TILE] = block.T
    work[...] = corr[...]
    count = work.shape[0]
    size = out.shape[2]
    pairs = TILE // (2 * size)
    for k in range(0, count, TILE):
        own_rows = slice(k, k + TILE)
        factor_tile(work, k)
        inverse = work[own_rows, own_rows]
        for side in (slice(0, k), slice(k + TILE, count)):
            if side.start < side.stop:
                work[own_rows, side] = dot32(inverse, work[own_rows, side], ((1,), (0,)))
        mine = [
            work[pl.ds(pl.multiple_of(k + 2 * i * size + core[0] * size, size), size), 0 : k + TILE]
            for i in range(pairs)
        ]
        turned = dot32(jnp.concatenate(mine, axis=0), fields[0 : k + TILE, :], ((1,), (0,)))
        for i in range(pairs):
            for t in range(out.shape[1]):
                out[k // TILE * pairs + i, t] = turned[i * size : (i + 1) * size, t * TILE : (t + 1) * TILE]
        for r in range(k + TILE, count, TILE):
            rows = slice(r, r + TILE)
            lower = work[own_rows, rows].T
            for side in (slice(r, count), slice(0, k)):
                if side.start < side.stop:
                    work[rows, side] = work[rows, side] - dot32(lower, work[own_rows, side], ((1,), (0,)))
            work[rows, own_rows] = -dot32(lower, inverse, ((1,), (0,)))


VMEM = pl.BlockSpec(memory_space=pltpu.VMEM)
SMEM = pl.BlockSpec(memory_space=pltpu.SMEM)
PARAMS = pltpu.CompilerParams(vmem_limit_bytes=48 << 20)


def flip(axes, bits):
    return [(i, i ^ bits) for i in range(lax.axis_size(axes))]


def per_device(orbitals, potential):
    planes, rows, cells = orbitals.shape
    side = lax.axis_index("xh")
    core = lax.axis_index("c").astype(jnp.int32).reshape(1)
    half = rows // 2
    own, other = (
        jnp.concatenate(
            [lax.dynamic_slice_in_dim(orbitals, at * half, half, 1).reshape(planes * half, cells), potential]
        )
        for at in (side, 1 - side)
    )
    slabs = lax.axis_size(SPACE)
    swap = [(s, s ^ 1) for s in range(slabs)]
    near = [(s, (s + 2 * (2 * (s % 2) - 1)) % slabs) for s in range(slabs)]
    cross = [(s, (s + 2 * (s % 2) - 1) % slabs) for s in range(slabs)]
    cross, swap, near = (
        lax.ppermute(x, SPACE, pairs) for x, pairs in ((other, cross), (other, swap), (own, near))
    )
    second = pl.pallas_call(
        functools.partial(filter_kernel, half, planes),
        out_shape=jax.ShapeDtypeStruct((4 * planes, half, TILE), jnp.float32),
        in_specs=[SMEM] + [VMEM] * 5,
        out_specs=VMEM,
        scratch_shapes=[pltpu.VMEM(((2 * planes + 2 * RADIUS) * half, cells), jnp.float32)],
        compiler_params=PARAMS,
        name="filter",
    )(side.astype(jnp.int32).reshape(1), own, swap, near, cross, jnp.asarray(plane_matrix()))

    team, layer = lax.axis_size(TEAM), lax.axis_size(LAYER)
    mine = lax.all_to_all(second.reshape(layer, 4 * planes // layer, half, TILE), LAYER, 0, 0)
    theirs = lax.ppermute(mine, ("c",), flip("c", 1))
    count = 2 * team * rows
    total = float(planes * lax.axis_size(SPACE) * cells)
    part, fields = pl.pallas_call(
        functools.partial(gram_kernel, 1.0 / total),
        out_shape=(
            jax.ShapeDtypeStruct((5 * TILE, TILE), jnp.float32),
            jax.ShapeDtypeStruct((count, mine.shape[1] * TILE), jnp.float32),
        ),
        in_specs=[SMEM, VMEM, VMEM],
        out_specs=(VMEM, VMEM),
        compiler_params=PARAMS,
        name="gram",
    )(core, mine, theirs)

    piece = lax.all_to_all(part.reshape(layer, 5 * TILE // layer, TILE), LAYER, 0, 0).sum(0)
    piece = piece + lax.ppermute(piece, "z", flip("z", 1))
    got = [lax.ppermute(piece, "z", flip("z", b)) for b in (2, 4, 6)]
    piece = (piece + got[0]) + (got[1] + got[2])
    spread = lax.all_to_all(jnp.broadcast_to(piece, (layer,) + piece.shape), LAYER, 0, 0)
    mine_g = spread.reshape(5 * TILE, TILE)
    theirs_g = lax.ppermute(mine_g, ("c",), flip("c", 1))
    correlation, turned = pl.pallas_call(
        factor_kernel,
        out_shape=(
            jax.ShapeDtypeStruct((count, count), jnp.float32),
            jax.ShapeDtypeStruct((team, mine.shape[1], rows, TILE), jnp.float32),
        ),
        in_specs=[SMEM, VMEM, VMEM, VMEM],
        out_specs=(VMEM, VMEM),
        scratch_shapes=[pltpu.VMEM((count, count), jnp.float32)],
        compiler_params=PARAMS,
        name="factor",
    )(core, mine_g, theirs_g, fields)
    back = lax.all_to_all(turned, TEAM, 0, 0).reshape(planes, 2, rows, TILE)
    return (back.transpose(0, 2, 1, 3).reshape(planes, rows, cells), correlation)


def solution(mesh):
    fine = Mesh(mesh.devices.reshape(8, 2, 4, 2, 2), ("z", "xh", "y", "xl", "c"))
    return jax.shard_map(
        per_device,
        mesh=fine,
        in_specs=(P(SPACE, BAND, None), P(SPACE, None)),
        out_specs=(P(SPACE, BAND, None), P()),
        check_vma=False,
    )
```

```python
import functools

import jax
import jax.numpy as jnp
import numpy as np
from jax import lax
from jax.experimental import pallas as pl
from jax.experimental.pallas import tpu as pltpu
from jax.sharding import Mesh
from jax.sharding import PartitionSpec as P

NX = 16
NY = 16
CELLS = NX * NY
COEFS = [12.0 / 7.0, -15.0 / 56.0, 10.0 / 189.0, -1.0 / 112.0, 2.0 / 1925.0, -1.0 / 16632.0]
CENTER_COEF = -5369.0 / 1800.0
INV_SPACING2 = 6.25
SHIFT_MID = 42.0
HALF_SPAN = 38.0
RADIUS = 6

SPACE = ("z", "xh")
TEAM = ("y", "xl")
LAYER = ("xh", "y", "xl")
BAND = ("y", "xl", "c")

BLOCKS = [[(0, 0), (1, 0), (1, 1), (2, 0), (2, 1)], [(2, 2), (3, 0), (3, 1), (3, 2), (3, 3)]]
TILE = 128
GROUP = 16

SCALE = -0.5 * INV_SPACING2 / HALF_SPAN


def plane_matrix():
    ring = np.zeros((NX, NX))
    for k, coef in enumerate(COEFS):
        for i in range(NX):
            ring[i, (i + k + 1) % NX] += coef
            ring[i, (i - k - 1) % NX] += coef
    one = np.eye(NX)
    full = np.kron(ring, one) + np.kron(one, ring) + 3.0 * CENTER_COEF * np.eye(CELLS)
    return (SCALE * full).astype(np.float32)


def dot32(a, b, dims):
    return lax.dot_general(
        a, b, (dims, ((), ())), precision=lax.Precision.HIGHEST, preferred_element_type=jnp.float32
    )


def filter_kernel(rows, planes, side, own, swap, near, cross, mat, out, first):
    size = planes * rows
    count = 2 * planes + 2 * RADIUS

    def filter_slabs(slabs):
        def field(p):
            return slabs[p // planes][p % planes * rows : (p % planes + 1) * rows, :]

        def level(p):
            at = size + p % planes
            return (slabs[p // planes][at : at + 1, :] - SHIFT_MID) / HALF_SPAN

        def plane(q):
            return first[q * rows : (q + 1) * rows, :]

        skip = planes - RADIUS
        for k, slab in enumerate(slabs):
            begin, end = max(k * planes, skip), min((k + 1) * planes, skip + count)
            part = slab[(begin - k * planes) * rows : (end - k * planes) * rows, :]
            first[(begin - skip) * rows : (end - skip) * rows, :] = dot32(part, mat[...], ((1,), (0,)))
        for q in range(count):
            p = q + skip
            acc = plane(q) + level(p) * field(p)
            for k in range(RADIUS):
                acc = acc + (SCALE * COEFS[k]) * (field(p + k + 1) + field(p - k - 1))
            first[q * rows : (q + 1) * rows, :] = acc
        inner = dot32(first[RADIUS * rows : RADIUS * rows + 2 * size, :], mat[...], ((1,), (0,)))
        for z in range(2 * planes):
            q = z + RADIUS
            acc = inner[z * rows : (z + 1) * rows, :] + level(z + planes) * plane(q)
            for k in range(RADIUS):
                acc = acc + (SCALE * COEFS[k]) * (plane(q + k + 1) + plane(q - k - 1))
            second = 2.0 * acc - field(z + planes)
            out[2 * z] = second[:, :TILE]
            out[2 * z + 1] = second[:, TILE:]

    @pl.when(side[0] == 0)
    def _():
        filter_slabs((cross, own, swap, near))

    @pl.when(side[0] == 1)
    def _():
        filter_slabs((near, swap, own, cross))


def gram_kernel(scale, core, own, other, out, stack):
    rows = own.shape[2]
    team = own.shape[0] // 2

    def gram_tiles(c):
        for half, ref in ((c, own), (1 - c, other)):
            for s in range(own.shape[0]):
                at = (s % team * 4 + half * 2 + s // team) * rows
                for t in range(own.shape[1]):
                    stack[at : at + rows, t * TILE : (t + 1) * TILE] = ref[s, t]
        for k, wide in ((0, 1), (1, 2), (3, 2)):
            i, j = BLOCKS[c][k]
            tiles = scale * dot32(
                stack[i * TILE : (i + 1) * TILE, :], stack[j * TILE : (j + wide) * TILE, :], ((1,), (1,))
            )
            for w in range(wide):
                out[(k + w) * TILE : (k + w + 1) * TILE, :] = tiles[:, w * TILE : (w + 1) * TILE]

    @pl.when(core[0] == 0)
    def _():
        gram_tiles(0)

    @pl.when(core[0] == 1)
    def _():
        gram_tiles(1)


def line(block, row):
    return jnp.broadcast_to(block[row : row + 1, :], (8, TILE))


def factor_tile(ref, origin):
    lane = lax.broadcasted_iota(jnp.int32, (8, TILE), 1)
    sub = lax.broadcasted_iota(jnp.int32, (8, TILE), 0)
    lanes = slice(origin, origin + TILE)
    halves = range(GROUP // 8)
    for base in range(0, TILE, GROUP):
        inside = (lane >= base) & (lane < base + GROUP)
        place = [slice(origin + base + 8 * h, origin + base + 8 * h + 8) for h in halves]
        rows = [ref[place[h], lanes] for h in halves]
        col = [
            [jnp.broadcast_to(rows[h][:, base + k : base + k + 1], (8, TILE)) for k in range(GROUP)]
            for h in halves
        ]
        start = [
            jnp.where(inside, jnp.where(lane - base == sub + 8 * h, 1.0, 0.0), rows[h]) for h in halves
        ]
        low, full = list(start), list(start)
        scale = [jnp.zeros((8, TILE), jnp.float32) for _ in halves]
        for j in range(GROUP):
            h, r = divmod(j, 8)
            at = sub == r
            pivot = line(col[h][j], r)
            inv = 1.0 / pivot
            scale[h] = jnp.where(at, lax.rsqrt(pivot), scale[h])
            mine = [col[i][j] for i in halves]
            for k in range(j + 1, GROUP):
                ratio = line(col[h][k], r) * inv
                for i in halves:
                    new = col[i][k] - mine[i] * ratio
                    col[i][k] = jnp.where(at, ratio, new) if i == h else new
            ratio = line(low[h], r) * inv
            for i in range(h, GROUP // 8):
                low[i] = low[i] - (jnp.where(sub > r, mine[i], 0.0) if i == h else mine[i]) * ratio
            ratio = line(full[h], r) * inv
            for i in halves:
                new = full[i] - mine[i] * ratio
                full[i] = jnp.where(at, ratio, new) if i == h else new
        for h in halves:
            ref[place[h], lanes] = jnp.where(lane < base + GROUP, low[h] * scale[h], 0.0)
        for q in range(base + GROUP, min(base + 2 * GROUP, TILE), 8):
            rest = ref[origin + q : origin + q + 8, lanes]
            acc = jnp.where(inside, 0.0, rest)
            for m in range(GROUP):
                acc = acc - jnp.broadcast_to(rest[:, base + m : base + m + 1], (8, TILE)) * line(
                    full[m // 8], m % 8
                )
            ref[origin + q : origin + q + 8, lanes] = acc
        if base + 2 * GROUP < TILE:
            far = slice(origin + base + 2 * GROUP, origin + TILE)
            rest = ref[far, lanes]
            column = lax.broadcasted_iota(jnp.int32, rest.shape, 1)
            among = (column >= base) & (column < base + GROUP)
            after = jnp.zeros((TILE - GROUP - base, TILE), jnp.float32)
            before = [jnp.zeros((base, TILE), jnp.float32)] if base else []
            spread = jnp.concatenate(before + full + [after], axis=0)
            ref[far, lanes] = jnp.where(among, 0.0, rest) - dot32(
                jnp.where(among, rest, 0.0), spread, ((1,), (0,))
            )


def factor_kernel(core, own, other, fields, corr_hbm, out, work, corr, sem):
    first = core[0] == 0
    for k in range(5):
        rows = slice(k * TILE, (k + 1) * TILE)
        a, b = own[rows, :], other[rows, :]
        for blocks, block in ((BLOCKS[0], jnp.where(first, a, b)), (BLOCKS[1], jnp.where(first, b, a))):
            i, j = blocks[k]
            corr[i * TILE : (i + 1) * TILE, j * TILE : (j + 1) * TILE] = block
            if i != j:
                corr[j * TILE : (j + 1) * TILE, i * TILE : (i + 1) * TILE] = block.T
    copy = pltpu.make_async_copy(corr, corr_hbm, sem)
    copy.start()
    work[...] = corr[...]
    count = work.shape[0]
    size = out.shape[2]
    pairs = TILE // (2 * size)
    for k in range(0, count, TILE):
        own_rows = slice(k, k + TILE)
        factor_tile(work, k)
        inverse = work[own_rows, own_rows]
        for side in (slice(0, k), slice(k + TILE, count)):
            if side.start < side.stop:
                work[own_rows, side] = dot32(inverse, work[own_rows, side], ((1,), (0,)))
        mine = [
            work[pl.ds(pl.multiple_of(k + 2 * i * size + core[0] * size, size), size), 0 : k + TILE]
            for i in range(pairs)
        ]
        turned = dot32(jnp.concatenate(mine, axis=0), fields[0 : k + TILE, :], ((1,), (0,)))
        for i in range(pairs):
            for t in range(out.shape[1]):
                out[k // TILE * pairs + i, t] = turned[i * size : (i + 1) * size, t * TILE : (t + 1) * TILE]
        for r in range(k + TILE, count, TILE):
            rows = slice(r, r + TILE)
            lower = work[own_rows, rows].T
            for side in (slice(r, count), slice(0, k)):
                if side.start < side.stop:
                    work[rows, side] = work[rows, side] - dot32(lower, work[own_rows, side], ((1,), (0,)))
            work[rows, own_rows] = -dot32(lower, inverse, ((1,), (0,)))
    copy.wait()


VMEM = pl.BlockSpec(memory_space=pltpu.VMEM)
SMEM = pl.BlockSpec(memory_space=pltpu.SMEM)
PARAMS = pltpu.CompilerParams(vmem_limit_bytes=48 << 20)


def flip(axes, bits):
    return [(i, i ^ bits) for i in range(lax.axis_size(axes))]


def per_device(orbitals, potential):
    planes, rows, cells = orbitals.shape
    side = lax.axis_index("xh")
    core = lax.axis_index("c").astype(jnp.int32).reshape(1)
    half = rows // 2
    own, other = (
        jnp.concatenate(
            [lax.dynamic_slice_in_dim(orbitals, at * half, half, 1).reshape(planes * half, cells), potential]
        )
        for at in (side, 1 - side)
    )
    slabs = lax.axis_size(SPACE)
    swap = [(s, s ^ 1) for s in range(slabs)]
    near = [(s, (s + 2 * (2 * (s % 2) - 1)) % slabs) for s in range(slabs)]
    cross = [(s, (s + 2 * (s % 2) - 1) % slabs) for s in range(slabs)]
    cross, swap, near = (
        lax.ppermute(x, SPACE, pairs) for x, pairs in ((other, cross), (other, swap), (own, near))
    )
    second = pl.pallas_call(
        functools.partial(filter_kernel, half, planes),
        out_shape=jax.ShapeDtypeStruct((4 * planes, half, TILE), jnp.float32),
        in_specs=[SMEM] + [VMEM] * 5,
        out_specs=VMEM,
        scratch_shapes=[pltpu.VMEM(((2 * planes + 2 * RADIUS) * half, cells), jnp.float32)],
        compiler_params=PARAMS,
        name="filter",
    )(side.astype(jnp.int32).reshape(1), own, swap, near, cross, jnp.asarray(plane_matrix()))

    team, layer = lax.axis_size(TEAM), lax.axis_size(LAYER)
    mine = lax.all_to_all(second.reshape(layer, 4 * planes // layer, half, TILE), LAYER, 0, 0)
    theirs = lax.ppermute(mine, ("c",), flip("c", 1))
    count = 2 * team * rows
    total = float(planes * lax.axis_size(SPACE) * cells)
    part, fields = pl.pallas_call(
        functools.partial(gram_kernel, 1.0 / total),
        out_shape=(
            jax.ShapeDtypeStruct((5 * TILE, TILE), jnp.float32),
            jax.ShapeDtypeStruct((count, mine.shape[1] * TILE), jnp.float32),
        ),
        in_specs=[SMEM, VMEM, VMEM],
        out_specs=(VMEM, VMEM),
        compiler_params=PARAMS,
        name="gram",
    )(core, mine, theirs)

    piece = lax.all_to_all(part.reshape(layer, 5 * TILE // layer, TILE), LAYER, 0, 0).sum(0)
    depth = lax.axis_size("z")
    piece = lax.all_to_all(jnp.broadcast_to(piece, (depth,) + piece.shape), "z", 0, 0).sum(0)
    spread = lax.all_to_all(jnp.broadcast_to(piece, (layer,) + piece.shape), LAYER, 0, 0)
    mine_g = spread.reshape(5 * TILE, TILE)
    theirs_g = lax.ppermute(mine_g, ("c",), flip("c", 1))
    correlation, turned = pl.pallas_call(
        factor_kernel,
        out_shape=(
            jax.ShapeDtypeStruct((count, count), jnp.float32),
            jax.ShapeDtypeStruct((team, mine.shape[1], rows, TILE), jnp.float32),
        ),
        in_specs=[SMEM, VMEM, VMEM, VMEM],
        out_specs=(pl.BlockSpec(memory_space=pl.ANY), VMEM),
        scratch_shapes=[
            pltpu.VMEM((count, count), jnp.float32),
            pltpu.VMEM((count, count), jnp.float32),
            pltpu.SemaphoreType.DMA,
        ],
        compiler_params=PARAMS,
        name="factor",
    )(core, mine_g, theirs_g, fields)
    back = lax.all_to_all(turned, TEAM, 0, 0).reshape(planes, 2, rows, TILE)
    return (back.transpose(0, 2, 1, 3).reshape(planes, rows, cells), correlation)


def solution(mesh):
    fine = Mesh(mesh.devices.reshape(8, 2, 4, 2, 2), ("z", "xh", "y", "xl", "c"))
    return jax.shard_map(
        per_device,
        mesh=fine,
        in_specs=(P(SPACE, BAND, None), P(SPACE, None)),
        out_specs=(P(SPACE, BAND, None), P()),
        check_vma=False,
    )
```

```python
import functools

import jax
import jax.numpy as jnp
import numpy as np
from jax import lax
from jax.experimental import pallas as pl
from jax.experimental.pallas import tpu as pltpu
from jax.sharding import Mesh
from jax.sharding import PartitionSpec as P

NX = 16
NY = 16
CELLS = NX * NY
COEFS = [12.0 / 7.0, -15.0 / 56.0, 10.0 / 189.0, -1.0 / 112.0, 2.0 / 1925.0, -1.0 / 16632.0]
CENTER_COEF = -5369.0 / 1800.0
INV_SPACING2 = 6.25
SHIFT_MID = 42.0
HALF_SPAN = 38.0
RADIUS = 6

SPACE = ("z", "xh")
TEAM = ("y", "xl")
LAYER = ("xh", "y", "xl")
BAND = ("y", "xl", "c")

BLOCKS = [[(0, 0), (1, 0), (1, 1), (2, 0), (2, 1)], [(2, 2), (3, 0), (3, 1), (3, 2), (3, 3)]]
TILE = 128
GROUP = 16

SCALE = -0.5 * INV_SPACING2 / HALF_SPAN


def plane_matrix():
    ring = np.zeros((NX, NX))
    for k, coef in enumerate(COEFS):
        for i in range(NX):
            ring[i, (i + k + 1) % NX] += coef
            ring[i, (i - k - 1) % NX] += coef
    one = np.eye(NX)
    full = np.kron(ring, one) + np.kron(one, ring) + 3.0 * CENTER_COEF * np.eye(CELLS)
    return (SCALE * full).astype(np.float32)


def dot32(a, b, dims):
    return lax.dot_general(
        a, b, (dims, ((), ())), precision=lax.Precision.HIGHEST, preferred_element_type=jnp.float32
    )


def filter_kernel(rows, planes, side, own, swap, near, cross, mat, out, first):
    size = planes * rows
    count = 2 * planes + 2 * RADIUS

    def filter_slabs(slabs):
        def field(p):
            return slabs[p // planes][p % planes * rows : (p % planes + 1) * rows, :]

        def level(p):
            at = size + p % planes
            return (slabs[p // planes][at : at + 1, :] - SHIFT_MID) / HALF_SPAN

        def plane(q):
            return first[q * rows : (q + 1) * rows, :]

        skip = planes - RADIUS
        for k, slab in enumerate(slabs):
            begin, end = max(k * planes, skip), min((k + 1) * planes, skip + count)
            part = slab[(begin - k * planes) * rows : (end - k * planes) * rows, :]
            first[(begin - skip) * rows : (end - skip) * rows, :] = dot32(part, mat[...], ((1,), (0,)))
        for q in range(count):
            p = q + skip
            acc = plane(q) + level(p) * field(p)
            for k in range(RADIUS):
                acc = acc + (SCALE * COEFS[k]) * (field(p + k + 1) + field(p - k - 1))
            first[q * rows : (q + 1) * rows, :] = acc
        inner = dot32(first[RADIUS * rows : RADIUS * rows + 2 * size, :], mat[...], ((1,), (0,)))
        for z in range(2 * planes):
            q = z + RADIUS
            acc = inner[z * rows : (z + 1) * rows, :] + level(z + planes) * plane(q)
            for k in range(RADIUS):
                acc = acc + (SCALE * COEFS[k]) * (plane(q + k + 1) + plane(q - k - 1))
            second = 2.0 * acc - field(z + planes)
            out[2 * z] = second[:, :TILE]
            out[2 * z + 1] = second[:, TILE:]

    @pl.when(side[0] == 0)
    def _():
        filter_slabs((cross, own, swap, near))

    @pl.when(side[0] == 1)
    def _():
        filter_slabs((near, swap, own, cross))


def gram_kernel(scale, core, own, other, out, stack):
    rows = own.shape[2]
    team = own.shape[0] // 2

    def gram_tiles(c):
        for half, ref in ((c, own), (1 - c, other)):
            for s in range(own.shape[0]):
                at = (s % team * 4 + half * 2 + s // team) * rows
                for t in range(own.shape[1]):
                    stack[at : at + rows, t * TILE : (t + 1) * TILE] = ref[s, t]
        for k, wide in ((0, 1), (1, 2), (3, 2)):
            i, j = BLOCKS[c][k]
            tiles = scale * dot32(
                stack[i * TILE : (i + 1) * TILE, :], stack[j * TILE : (j + wide) * TILE, :], ((1,), (1,))
            )
            for w in range(wide):
                out[(k + w) * TILE : (k + w + 1) * TILE, :] = tiles[:, w * TILE : (w + 1) * TILE]

    @pl.when(core[0] == 0)
    def _():
        gram_tiles(0)

    @pl.when(core[0] == 1)
    def _():
        gram_tiles(1)


def line(block, row):
    return jnp.broadcast_to(block[row : row + 1, :], (8, TILE))


def factor_tile(ref, origin):
    lane = lax.broadcasted_iota(jnp.int32, (8, TILE), 1)
    sub = lax.broadcasted_iota(jnp.int32, (8, TILE), 0)
    lanes = slice(origin, origin + TILE)
    halves = range(GROUP // 8)
    for base in range(0, TILE, GROUP):
        inside = (lane >= base) & (lane < base + GROUP)
        place = [slice(origin + base + 8 * h, origin + base + 8 * h + 8) for h in halves]
        rows = [ref[place[h], lanes] for h in halves]
        col = [
            [jnp.broadcast_to(rows[h][:, base + k : base + k + 1], (8, TILE)) for k in range(GROUP)]
            for h in halves
        ]
        start = [
            jnp.where(inside, jnp.where(lane - base == sub + 8 * h, 1.0, 0.0), rows[h]) for h in halves
        ]
        low, full = list(start), list(start)
        scale = [jnp.zeros((8, TILE), jnp.float32) for _ in halves]
        for j in range(GROUP):
            h, r = divmod(j, 8)
            at = sub == r
            pivot = line(col[h][j], r)
            inv = 1.0 / pivot
            scale[h] = jnp.where(at, lax.rsqrt(pivot), scale[h])
            mine = [col[i][j] for i in halves]
            for k in range(j + 1, GROUP):
                ratio = line(col[h][k], r) * inv
                for i in halves:
                    new = col[i][k] - mine[i] * ratio
                    col[i][k] = jnp.where(at, ratio, new) if i == h else new
            ratio = line(low[h], r) * inv
            for i in range(h, GROUP // 8):
                low[i] = low[i] - (jnp.where(sub > r, mine[i], 0.0) if i == h else mine[i]) * ratio
            ratio = line(full[h], r) * inv
            for i in halves:
                new = full[i] - mine[i] * ratio
                full[i] = jnp.where(at, ratio, new) if i == h else new
        for h in halves:
            ref[place[h], lanes] = jnp.where(lane < base + GROUP, low[h] * scale[h], 0.0)
        for q in range(base + GROUP, min(base + 2 * GROUP, TILE), 8):
            rest = ref[origin + q : origin + q + 8, lanes]
            acc = jnp.where(inside, 0.0, rest)
            for m in range(GROUP):
                acc = acc - jnp.broadcast_to(rest[:, base + m : base + m + 1], (8, TILE)) * line(
                    full[m // 8], m % 8
                )
            ref[origin + q : origin + q + 8, lanes] = acc
        if base + 2 * GROUP < TILE:
            far = slice(origin + base + 2 * GROUP, origin + TILE)
            rest = ref[far, lanes]
            column = lax.broadcasted_iota(jnp.int32, rest.shape, 1)
            among = (column >= base) & (column < base + GROUP)
            after = jnp.zeros((TILE - GROUP - base, TILE), jnp.float32)
            before = [jnp.zeros((base, TILE), jnp.float32)] if base else []
            spread = jnp.concatenate(before + full + [after], axis=0)
            ref[far, lanes] = jnp.where(among, 0.0, rest) - dot32(
                jnp.where(among, rest, 0.0), spread, ((1,), (0,))
            )


def factor_kernel(core, own, other, fields, corr_hbm, out, work, corr, sem):
    first = core[0] == 0
    for k in range(5):
        rows = slice(k * TILE, (k + 1) * TILE)
        a, b = own[rows, :], other[rows, :]
        for blocks, block in ((BLOCKS[0], jnp.where(first, a, b)), (BLOCKS[1], jnp.where(first, b, a))):
            i, j = blocks[k]
            corr[i * TILE : (i + 1) * TILE, j * TILE : (j + 1) * TILE] = block
            if i != j:
                corr[j * TILE : (j + 1) * TILE, i * TILE : (i + 1) * TILE] = block.T
    copy = pltpu.make_async_copy(corr, corr_hbm, sem)
    copy.start()
    work[...] = corr[...]
    count = work.shape[0]
    size = out.shape[2]
    pairs = TILE // (2 * size)

    def own_part(k, columns):
        picked = []
        for at in range(k, k + TILE, 2 * size):
            picked.append(
                jnp.where(first, work[at : at + size, columns], work[at + size : at + 2 * size, columns])
            )
        return jnp.concatenate(picked, axis=0)

    def put(k, turned):
        for i in range(pairs):
            for t in range(out.shape[1]):
                out[k // TILE * pairs + i, t] = turned[i * size : (i + 1) * size, t * TILE : (t + 1) * TILE]

    def next_tile(k):
        here, after = slice(k, k + TILE), slice(k + TILE, k + 2 * TILE)
        upper = dot32(work[here, here], work[here, after], ((1,), (0,)))
        work[here, after] = upper
        work[after, after] = work[after, after] - dot32(upper.T, upper, ((1,), (0,)))

    def other_tiles(k):
        here = slice(k, k + TILE)
        inverse = work[here, here]
        for side in (slice(k + 2 * TILE, count), slice(0, k)):
            if side.start < side.stop:
                work[here, side] = dot32(inverse, work[here, side], ((1,), (0,)))
        for r in range(k + TILE, count, TILE):
            rows = slice(r, r + TILE)
            lower = work[here, rows].T
            for side in (slice(r + TILE if r == k + TILE else r, count), slice(0, k)):
                if side.start < side.stop:
                    work[rows, side] = work[rows, side] - dot32(lower, work[here, side], ((1,), (0,)))
            work[rows, here] = -dot32(lower, inverse, ((1,), (0,)))
        done = slice(0, k + TILE)
        put(k, dot32(own_part(k, done), fields[done, :], ((1,), (0,))))

    for k in range(0, count, TILE):
        factor_tile(work, k)
        if k:
            other_tiles(k - TILE)
        if k + TILE < count:
            next_tile(k)
    last = slice(k, count)
    summed = dot32(work[last, 0:k], fields[0:k, :], ((1,), (0,))) + fields[last, :]
    put(k, dot32(own_part(k, last), summed, ((1,), (0,))))
    copy.wait()


VMEM = pl.BlockSpec(memory_space=pltpu.VMEM)
SMEM = pl.BlockSpec(memory_space=pltpu.SMEM)
PARAMS = pltpu.CompilerParams(vmem_limit_bytes=48 << 20)


def flip(axes, bits):
    return [(i, i ^ bits) for i in range(lax.axis_size(axes))]


def per_device(orbitals, potential):
    planes, rows, cells = orbitals.shape
    side = lax.axis_index("xh")
    core = lax.axis_index("c").astype(jnp.int32).reshape(1)
    half = rows // 2
    own, other = (
        jnp.concatenate(
            [lax.dynamic_slice_in_dim(orbitals, at * half, half, 1).reshape(planes * half, cells), potential]
        )
        for at in (side, 1 - side)
    )
    slabs = lax.axis_size(SPACE)
    swap = [(s, s ^ 1) for s in range(slabs)]
    near = [(s, (s + 2 * (2 * (s % 2) - 1)) % slabs) for s in range(slabs)]
    cross = [(s, (s + 2 * (s % 2) - 1) % slabs) for s in range(slabs)]
    cross, swap, near = (
        lax.ppermute(x, SPACE, pairs) for x, pairs in ((other, cross), (other, swap), (own, near))
    )
    second = pl.pallas_call(
        functools.partial(filter_kernel, half, planes),
        out_shape=jax.ShapeDtypeStruct((4 * planes, half, TILE), jnp.float32),
        in_specs=[SMEM] + [VMEM] * 5,
        out_specs=VMEM,
        scratch_shapes=[pltpu.VMEM(((2 * planes + 2 * RADIUS) * half, cells), jnp.float32)],
        compiler_params=PARAMS,
        name="filter",
    )(side.astype(jnp.int32).reshape(1), own, swap, near, cross, jnp.asarray(plane_matrix()))

    team, layer = lax.axis_size(TEAM), lax.axis_size(LAYER)
    mine = lax.all_to_all(second.reshape(layer, 4 * planes // layer, half, TILE), LAYER, 0, 0)
    theirs = lax.ppermute(mine, ("c",), flip("c", 1))
    count = 2 * team * rows
    total = float(planes * lax.axis_size(SPACE) * cells)
    part, fields = pl.pallas_call(
        functools.partial(gram_kernel, 1.0 / total),
        out_shape=(
            jax.ShapeDtypeStruct((5 * TILE, TILE), jnp.float32),
            jax.ShapeDtypeStruct((count, mine.shape[1] * TILE), jnp.float32),
        ),
        in_specs=[SMEM, VMEM, VMEM],
        out_specs=(VMEM, VMEM),
        compiler_params=PARAMS,
        name="gram",
    )(core, mine, theirs)

    piece = lax.all_to_all(part.reshape(layer, 5 * TILE // layer, TILE), LAYER, 0, 0).sum(0)
    depth = lax.axis_size("z")
    piece = lax.all_to_all(jnp.broadcast_to(piece, (depth,) + piece.shape), "z", 0, 0).sum(0)
    spread = lax.all_to_all(jnp.broadcast_to(piece, (layer,) + piece.shape), LAYER, 0, 0)
    mine_g = spread.reshape(5 * TILE, TILE)
    theirs_g = lax.ppermute(mine_g, ("c",), flip("c", 1))
    correlation, turned = pl.pallas_call(
        factor_kernel,
        out_shape=(
            jax.ShapeDtypeStruct((count, count), jnp.float32),
            jax.ShapeDtypeStruct((team, mine.shape[1], rows, TILE), jnp.float32),
        ),
        in_specs=[SMEM, VMEM, VMEM, VMEM],
        out_specs=(pl.BlockSpec(memory_space=pl.ANY), VMEM),
        scratch_shapes=[
            pltpu.VMEM((count, count), jnp.float32),
            pltpu.VMEM((count, count), jnp.float32),
            pltpu.SemaphoreType.DMA,
        ],
        compiler_params=PARAMS,
        name="factor",
    )(core, mine_g, theirs_g, fields)
    back = lax.all_to_all(turned, TEAM, 0, 0).reshape(planes, 2, rows, TILE)
    return (back.transpose(0, 2, 1, 3).reshape(planes, rows, cells), correlation)


def solution(mesh):
    fine = Mesh(mesh.devices.reshape(8, 2, 4, 2, 2), ("z", "xh", "y", "xl", "c"))
    return jax.shard_map(
        per_device,
        mesh=fine,
        in_specs=(P(SPACE, BAND, None), P(SPACE, None)),
        out_specs=(P(SPACE, BAND, None), P()),
        check_vma=False,
    )
```

```python
import functools

import jax
import jax.numpy as jnp
import numpy as np
from jax import lax
from jax.experimental import pallas as pl
from jax.experimental.pallas import tpu as pltpu
from jax.sharding import Mesh
from jax.sharding import PartitionSpec as P

NX = 16
NY = 16
CELLS = NX * NY
COEFS = [12.0 / 7.0, -15.0 / 56.0, 10.0 / 189.0, -1.0 / 112.0, 2.0 / 1925.0, -1.0 / 16632.0]
CENTER_COEF = -5369.0 / 1800.0
INV_SPACING2 = 6.25
SHIFT_MID = 42.0
HALF_SPAN = 38.0
RADIUS = 6

SPACE = ("z", "xh")
TEAM = ("y", "xl")
LAYER = ("xh", "y", "xl")
BAND = ("y", "xl", "c")

BLOCKS = [[(0, 0), (1, 0), (1, 1), (2, 0), (2, 1)], [(2, 2), (3, 0), (3, 1), (3, 2), (3, 3)]]
TILE = 128
GROUP = 16

SCALE = -0.5 * INV_SPACING2 / HALF_SPAN


def plane_matrix():
    ring = np.zeros((NX, NX))
    for k, coef in enumerate(COEFS):
        for i in range(NX):
            ring[i, (i + k + 1) % NX] += coef
            ring[i, (i - k - 1) % NX] += coef
    one = np.eye(NX)
    full = np.kron(ring, one) + np.kron(one, ring) + 3.0 * CENTER_COEF * np.eye(CELLS)
    return (SCALE * full).astype(np.float32)


def dot32(a, b, dims):
    return lax.dot_general(
        a, b, (dims, ((), ())), precision=lax.Precision.HIGHEST, preferred_element_type=jnp.float32
    )


def filter_kernel(rows, planes, side, own, swap, near, cross, mat, out, first):
    size = planes * rows
    count = 2 * planes + 2 * RADIUS

    def filter_slabs(slabs):
        def field(p):
            return slabs[p // planes][p % planes * rows : (p % planes + 1) * rows, :]

        def level(p):
            at = size + p % planes
            return (slabs[p // planes][at : at + 1, :] - SHIFT_MID) / HALF_SPAN

        def plane(q):
            return first[q * rows : (q + 1) * rows, :]

        skip = planes - RADIUS
        for k, slab in enumerate(slabs):
            begin, end = max(k * planes, skip), min((k + 1) * planes, skip + count)
            part = slab[(begin - k * planes) * rows : (end - k * planes) * rows, :]
            first[(begin - skip) * rows : (end - skip) * rows, :] = dot32(part, mat[...], ((1,), (0,)))
        for q in range(count):
            p = q + skip
            acc = plane(q) + level(p) * field(p)
            for k in range(RADIUS):
                acc = acc + (SCALE * COEFS[k]) * (field(p + k + 1) + field(p - k - 1))
            first[q * rows : (q + 1) * rows, :] = acc
        inner = dot32(first[RADIUS * rows : RADIUS * rows + 2 * size, :], mat[...], ((1,), (0,)))
        for z in range(2 * planes):
            q = z + RADIUS
            acc = inner[z * rows : (z + 1) * rows, :] + level(z + planes) * plane(q)
            for k in range(RADIUS):
                acc = acc + (SCALE * COEFS[k]) * (plane(q + k + 1) + plane(q - k - 1))
            second = 2.0 * acc - field(z + planes)
            out[2 * z] = second[:, :TILE]
            out[2 * z + 1] = second[:, TILE:]

    @pl.when(side[0] == 0)
    def _():
        filter_slabs((cross, own, swap, near))

    @pl.when(side[0] == 1)
    def _():
        filter_slabs((near, swap, own, cross))


def gram_kernel(scale, core, own, other, out, stack):
    rows = own.shape[2]
    team = own.shape[0] // 2

    def gram_tiles(c):
        for half, ref in ((c, own), (1 - c, other)):
            for s in range(own.shape[0]):
                at = (s % team * 4 + half * 2 + s // team) * rows
                for t in range(own.shape[1]):
                    stack[at : at + rows, t * TILE : (t + 1) * TILE] = ref[s, t]
        for k, wide in ((0, 1), (1, 2), (3, 2)):
            i, j = BLOCKS[c][k]
            tiles = scale * dot32(
                stack[i * TILE : (i + 1) * TILE, :], stack[j * TILE : (j + wide) * TILE, :], ((1,), (1,))
            )
            for w in range(wide):
                out[(k + w) * TILE : (k + w + 1) * TILE, :] = tiles[:, w * TILE : (w + 1) * TILE]

    @pl.when(core[0] == 0)
    def _():
        gram_tiles(0)

    @pl.when(core[0] == 1)
    def _():
        gram_tiles(1)


def line(block, row):
    return jnp.broadcast_to(block[row : row + 1, :], (8, TILE))


def factor_tile(ref, origin):
    lane = lax.broadcasted_iota(jnp.int32, (8, TILE), 1)
    sub = lax.broadcasted_iota(jnp.int32, (8, TILE), 0)
    lanes = slice(origin, origin + TILE)
    halves = range(GROUP // 8)
    for base in range(0, TILE, GROUP):
        inside = (lane >= base) & (lane < base + GROUP)
        place = [slice(origin + base + 8 * h, origin + base + 8 * h + 8) for h in halves]
        rows = [ref[place[h], lanes] for h in halves]
        col = [
            [jnp.broadcast_to(rows[h][:, base + k : base + k + 1], (8, TILE)) for k in range(GROUP)]
            for h in halves
        ]
        start = [
            jnp.where(inside, jnp.where(lane - base == sub + 8 * h, 1.0, 0.0), rows[h]) for h in halves
        ]
        low, full = list(start), list(start)
        scale = [jnp.zeros((8, TILE), jnp.float32) for _ in halves]
        for j in range(GROUP):
            h, r = divmod(j, 8)
            at = sub == r
            pivot = line(col[h][j], r)
            inv = 1.0 / pivot
            scale[h] = jnp.where(at, lax.rsqrt(pivot), scale[h])
            mine = [col[i][j] for i in halves]
            for k in range(j + 1, GROUP):
                ratio = line(col[h][k], r) * inv
                for i in halves:
                    new = col[i][k] - mine[i] * ratio
                    col[i][k] = jnp.where(at, ratio, new) if i == h else new
            ratio = line(low[h], r) * inv
            for i in range(h, GROUP // 8):
                low[i] = low[i] - (jnp.where(sub > r, mine[i], 0.0) if i == h else mine[i]) * ratio
            ratio = line(full[h], r) * inv
            for i in halves:
                new = full[i] - mine[i] * ratio
                full[i] = jnp.where(at, ratio, new) if i == h else new
        for h in halves:
            ref[place[h], lanes] = jnp.where(lane < base + GROUP, low[h] * scale[h], 0.0)
        for q in range(base + GROUP, min(base + 2 * GROUP, TILE), 8):
            rest = ref[origin + q : origin + q + 8, lanes]
            acc = jnp.where(inside, 0.0, rest)
            for m in range(GROUP):
                acc = acc - jnp.broadcast_to(rest[:, base + m : base + m + 1], (8, TILE)) * line(
                    full[m // 8], m % 8
                )
            ref[origin + q : origin + q + 8, lanes] = acc
        if base + 2 * GROUP < TILE:
            far = slice(origin + base + 2 * GROUP, origin + TILE)
            rest = ref[far, lanes]
            column = lax.broadcasted_iota(jnp.int32, rest.shape, 1)
            among = (column >= base) & (column < base + GROUP)
            after = jnp.zeros((TILE - GROUP - base, TILE), jnp.float32)
            before = [jnp.zeros((base, TILE), jnp.float32)] if base else []
            spread = jnp.concatenate(before + full + [after], axis=0)
            ref[far, lanes] = jnp.where(among, 0.0, rest) - dot32(
                jnp.where(among, rest, 0.0), spread, ((1,), (0,))
            )


def factor_kernel(core, own, other, fields, corr_hbm, out, work, corr, sem):
    first = core[0] == 0

    count = work.shape[0]
    size = out.shape[2]
    pairs = TILE // (2 * size)

    def own_part(k, columns):
        picked = []
        for at in range(k, k + TILE, 2 * size):
            picked.append(
                jnp.where(first, work[at : at + size, columns], work[at + size : at + 2 * size, columns])
            )
        return jnp.concatenate(picked, axis=0)

    def put(k, turned):
        for i in range(pairs):
            for t in range(out.shape[1]):
                out[k // TILE * pairs + i, t] = turned[i * size : (i + 1) * size, t * TILE : (t + 1) * TILE]

    def join():
        for k in range(5):
            rows = slice(k * TILE, (k + 1) * TILE)
            a, b = own[rows, :], other[rows, :]
            for blocks, block in (
                (BLOCKS[0], jnp.where(first, a, b)),
                (BLOCKS[1], jnp.where(first, b, a)),
            ):
                i, j = (slice(t * TILE, (t + 1) * TILE) for t in blocks[k])
                corr[i, j] = block
                if i != j:
                    turned = block.T
                    corr[j, i] = turned
                    work[j, i] = turned
                if j.start or i.start:
                    work[i, j] = block

    def next_tile(k):
        here, after = slice(k, k + TILE), slice(k + TILE, k + 2 * TILE)
        upper = dot32(work[here, here], work[here, after], ((1,), (0,)))
        work[here, after] = upper
        work[after, after] = work[after, after] - dot32(upper.T, upper, ((1,), (0,)))

    def other_tiles(k):
        here = slice(k, k + TILE)
        inverse = work[here, here]
        for side in (slice(k + 2 * TILE, count), slice(0, k)):
            if side.start < side.stop:
                work[here, side] = dot32(inverse, work[here, side], ((1,), (0,)))
        for r in range(k + TILE, count, TILE):
            rows = slice(r, r + TILE)
            lower = work[here, rows].T
            for side in (slice(r + TILE if r == k + TILE else r, count), slice(0, k)):
                if side.start < side.stop:
                    work[rows, side] = work[rows, side] - dot32(lower, work[here, side], ((1,), (0,)))
            work[rows, here] = -dot32(lower, inverse, ((1,), (0,)))
        done = slice(0, k + TILE)
        put(k, dot32(own_part(k, done), fields[done, :], ((1,), (0,))))

    work[0:TILE, 0:TILE] = jnp.where(first, own[0:TILE, :], other[0:TILE, :])
    for k in range(0, count, TILE):
        factor_tile(work, k)
        if k:
            other_tiles(k - TILE)
        else:
            join()
            copy = pltpu.make_async_copy(corr, corr_hbm, sem)
            copy.start()
        if k + TILE < count:
            next_tile(k)
    last = slice(k, count)
    summed = dot32(work[last, 0:k], fields[0:k, :], ((1,), (0,))) + fields[last, :]
    put(k, dot32(own_part(k, last), summed, ((1,), (0,))))
    copy.wait()


VMEM = pl.BlockSpec(memory_space=pltpu.VMEM)
SMEM = pl.BlockSpec(memory_space=pltpu.SMEM)
PARAMS = pltpu.CompilerParams(vmem_limit_bytes=48 << 20)


def flip(axes, bits):
    return [(i, i ^ bits) for i in range(lax.axis_size(axes))]


def per_device(orbitals, potential):
    planes, rows, cells = orbitals.shape
    side = lax.axis_index("xh")
    core = lax.axis_index("c").astype(jnp.int32).reshape(1)
    half = rows // 2
    own, other = (
        jnp.concatenate(
            [lax.dynamic_slice_in_dim(orbitals, at * half, half, 1).reshape(planes * half, cells), potential]
        )
        for at in (side, 1 - side)
    )
    slabs = lax.axis_size(SPACE)
    swap = [(s, s ^ 1) for s in range(slabs)]
    near = [(s, (s + 2 * (2 * (s % 2) - 1)) % slabs) for s in range(slabs)]
    cross = [(s, (s + 2 * (s % 2) - 1) % slabs) for s in range(slabs)]
    cross, swap, near = (
        lax.ppermute(x, SPACE, pairs) for x, pairs in ((other, cross), (other, swap), (own, near))
    )
    second = pl.pallas_call(
        functools.partial(filter_kernel, half, planes),
        out_shape=jax.ShapeDtypeStruct((4 * planes, half, TILE), jnp.float32),
        in_specs=[SMEM] + [VMEM] * 5,
        out_specs=VMEM,
        scratch_shapes=[pltpu.VMEM(((2 * planes + 2 * RADIUS) * half, cells), jnp.float32)],
        compiler_params=PARAMS,
        name="filter",
    )(side.astype(jnp.int32).reshape(1), own, swap, near, cross, jnp.asarray(plane_matrix()))

    team, layer = lax.axis_size(TEAM), lax.axis_size(LAYER)
    mine = lax.all_to_all(second.reshape(layer, 4 * planes // layer, half, TILE), LAYER, 0, 0)
    theirs = lax.ppermute(mine, ("c",), flip("c", 1))
    count = 2 * team * rows
    total = float(planes * lax.axis_size(SPACE) * cells)
    part, fields = pl.pallas_call(
        functools.partial(gram_kernel, 1.0 / total),
        out_shape=(
            jax.ShapeDtypeStruct((5 * TILE, TILE), jnp.float32),
            jax.ShapeDtypeStruct((count, mine.shape[1] * TILE), jnp.float32),
        ),
        in_specs=[SMEM, VMEM, VMEM],
        out_specs=(VMEM, VMEM),
        compiler_params=PARAMS,
        name="gram",
    )(core, mine, theirs)

    piece = lax.all_to_all(part.reshape(layer, 5 * TILE // layer, TILE), LAYER, 0, 0).sum(0)
    depth = lax.axis_size("z")
    piece = lax.all_to_all(jnp.broadcast_to(piece, (depth,) + piece.shape), "z", 0, 0).sum(0)
    spread = lax.all_to_all(jnp.broadcast_to(piece, (layer,) + piece.shape), LAYER, 0, 0)
    mine_g = spread.reshape(5 * TILE, TILE)
    theirs_g = lax.ppermute(mine_g, ("c",), flip("c", 1))
    correlation, turned = pl.pallas_call(
        factor_kernel,
        out_shape=(
            jax.ShapeDtypeStruct((count, count), jnp.float32),
            jax.ShapeDtypeStruct((team, mine.shape[1], rows, TILE), jnp.float32),
        ),
        in_specs=[SMEM, VMEM, VMEM, VMEM],
        out_specs=(pl.BlockSpec(memory_space=pl.ANY), VMEM),
        scratch_shapes=[
            pltpu.VMEM((count, count), jnp.float32),
            pltpu.VMEM((count, count), jnp.float32),
            pltpu.SemaphoreType.DMA,
        ],
        compiler_params=PARAMS,
        name="factor",
    )(core, mine_g, theirs_g, fields)
    back = lax.all_to_all(turned, TEAM, 0, 0).reshape(planes, 2, rows, TILE)
    return (back.transpose(0, 2, 1, 3).reshape(planes, rows, cells), correlation)


def solution(mesh):
    fine = Mesh(mesh.devices.reshape(8, 2, 4, 2, 2), ("z", "xh", "y", "xl", "c"))
    return jax.shard_map(
        per_device,
        mesh=fine,
        in_specs=(P(SPACE, BAND, None), P(SPACE, None)),
        out_specs=(P(SPACE, BAND, None), P()),
        check_vma=False,
    )
```

```python
import functools

import jax
import jax.numpy as jnp
import numpy as np
from jax import lax
from jax.experimental import pallas as pl
from jax.experimental.pallas import tpu as pltpu
from jax.sharding import Mesh
from jax.sharding import PartitionSpec as P

NX = 16
NY = 16
CELLS = NX * NY
COEFS = [12.0 / 7.0, -15.0 / 56.0, 10.0 / 189.0, -1.0 / 112.0, 2.0 / 1925.0, -1.0 / 16632.0]
CENTER_COEF = -5369.0 / 1800.0
INV_SPACING2 = 6.25
SHIFT_MID = 42.0
HALF_SPAN = 38.0
RADIUS = 6

SPACE = ("z", "xh")
TEAM = ("y", "xl")
LAYER = ("xh", "y", "xl")
BAND = ("y", "xl", "c")

BLOCKS = [[(0, 0), (1, 0), (1, 1), (2, 0), (2, 1)], [(2, 2), (3, 0), (3, 1), (3, 2), (3, 3)]]
TILE = 128
GROUP = 16

SCALE = -0.5 * INV_SPACING2 / HALF_SPAN


def plane_matrix():
    ring = np.zeros((NX, NX))
    for k, coef in enumerate(COEFS):
        for i in range(NX):
            ring[i, (i + k + 1) % NX] += coef
            ring[i, (i - k - 1) % NX] += coef
    one = np.eye(NX)
    full = np.kron(ring, one) + np.kron(one, ring) + 3.0 * CENTER_COEF * np.eye(CELLS)
    return (SCALE * full).astype(np.float32)


def dot32(a, b, dims):
    return lax.dot_general(
        a, b, (dims, ((), ())), precision=lax.Precision.HIGHEST, preferred_element_type=jnp.float32
    )


def filter_kernel(rows, planes, side, own, swap, near, cross, mat, out, first):
    size = planes * rows
    count = 2 * planes + 2 * RADIUS

    def filter_slabs(slabs):
        def field(p, r, lanes):
            at = p % planes * rows + r
            return slabs[p // planes][at : at + 8, lanes]

        def level(p, lanes):
            at = size + p % planes
            return (slabs[p // planes][at : at + 1, lanes] - SHIFT_MID) / HALF_SPAN

        skip = planes - RADIUS
        for k, slab in enumerate(slabs):
            begin, end = max(k * planes, skip), min((k + 1) * planes, skip + count)
            part = slab[(begin - k * planes) * rows : (end - k * planes) * rows, :]
            first[(begin - skip) * rows : (end - skip) * rows, :] = dot32(part, mat[...], ((1,), (0,)))
        places = [(r, slice(l, l + TILE)) for r in range(0, rows, 8) for l in range(0, CELLS, TILE)]
        for r, lanes in places:
            for q in range(count):
                p = q + skip
                at = slice(q * rows + r, q * rows + r + 8)
                acc = first[at, lanes] + level(p, lanes) * field(p, r, lanes)
                for k in range(RADIUS):
                    acc = acc + (SCALE * COEFS[k]) * (field(p + k + 1, r, lanes) + field(p - k - 1, r, lanes))
                first[at, lanes] = acc
        inner = dot32(first[RADIUS * rows : RADIUS * rows + 2 * size, :], mat[...], ((1,), (0,)))
        for r, lanes in places:
            window = [first[q * rows + r : q * rows + r + 8, lanes] for q in range(count)]
            for z in range(2 * planes):
                q = z + RADIUS
                acc = inner[z * rows + r : z * rows + r + 8, lanes] + level(z + planes, lanes) * window[q]
                for k in range(RADIUS):
                    acc = acc + (SCALE * COEFS[k]) * (window[q + k + 1] + window[q - k - 1])
                second = 2.0 * acc - field(z + planes, r, lanes)
                out[2 * z + lanes.start // TILE, r : r + 8, :] = second

    @pl.when(side[0] == 0)
    def _():
        filter_slabs((cross, own, swap, near))

    @pl.when(side[0] == 1)
    def _():
        filter_slabs((near, swap, own, cross))


def gram_kernel(scale, core, own, other, out, stack):
    rows = own.shape[2]
    team = own.shape[0] // 2

    def gram_tiles(c):
        for half, ref in ((c, own), (1 - c, other)):
            for s in range(own.shape[0]):
                at = (s % team * 4 + half * 2 + s // team) * rows
                for t in range(own.shape[1]):
                    stack[at : at + rows, t * TILE : (t + 1) * TILE] = ref[s, t]
        for k, wide in ((0, 1), (1, 2), (3, 2)):
            i, j = BLOCKS[c][k]
            tiles = scale * dot32(
                stack[i * TILE : (i + 1) * TILE, :], stack[j * TILE : (j + wide) * TILE, :], ((1,), (1,))
            )
            for w in range(wide):
                out[(k + w) * TILE : (k + w + 1) * TILE, :] = tiles[:, w * TILE : (w + 1) * TILE]

    @pl.when(core[0] == 0)
    def _():
        gram_tiles(0)

    @pl.when(core[0] == 1)
    def _():
        gram_tiles(1)


def line(block, row):
    return jnp.broadcast_to(block[row : row + 1, :], (8, TILE))


def factor_tile(ref, origin):
    lane = lax.broadcasted_iota(jnp.int32, (8, TILE), 1)
    sub = lax.broadcasted_iota(jnp.int32, (8, TILE), 0)
    lanes = slice(origin, origin + TILE)
    halves = range(GROUP // 8)
    for base in range(0, TILE, GROUP):
        inside = (lane >= base) & (lane < base + GROUP)
        place = [slice(origin + base + 8 * h, origin + base + 8 * h + 8) for h in halves]
        rows = [ref[place[h], lanes] for h in halves]
        col = [
            [jnp.broadcast_to(rows[h][:, base + k : base + k + 1], (8, TILE)) for k in range(GROUP)]
            for h in halves
        ]
        start = [
            jnp.where(inside, jnp.where(lane - base == sub + 8 * h, 1.0, 0.0), rows[h]) for h in halves
        ]
        low, full = list(start), list(start)
        scale = [jnp.zeros((8, TILE), jnp.float32) for _ in halves]
        for j in range(GROUP):
            h, r = divmod(j, 8)
            at = sub == r
            pivot = line(col[h][j], r)
            inv = 1.0 / pivot
            scale[h] = jnp.where(at, lax.rsqrt(pivot), scale[h])
            mine = [col[i][j] for i in halves]
            for k in range(j + 1, GROUP):
                ratio = line(col[h][k], r) * inv
                for i in halves:
                    new = col[i][k] - mine[i] * ratio
                    col[i][k] = jnp.where(at, ratio, new) if i == h else new
            ratio = line(low[h], r) * inv
            for i in range(h, GROUP // 8):
                low[i] = low[i] - (jnp.where(sub > r, mine[i], 0.0) if i == h else mine[i]) * ratio
            ratio = line(full[h], r) * inv
            for i in halves:
                new = full[i] - mine[i] * ratio
                full[i] = jnp.where(at, ratio, new) if i == h else new
        for h in halves:
            ref[place[h], lanes] = jnp.where(lane < base + GROUP, low[h] * scale[h], 0.0)
        for q in range(base + GROUP, min(base + 2 * GROUP, TILE), 8):
            rest = ref[origin + q : origin + q + 8, lanes]
            acc = jnp.where(inside, 0.0, rest)
            for m in range(GROUP):
                acc = acc - jnp.broadcast_to(rest[:, base + m : base + m + 1], (8, TILE)) * line(
                    full[m // 8], m % 8
                )
            ref[origin + q : origin + q + 8, lanes] = acc
        if base + 2 * GROUP < TILE:
            far = slice(origin + base + 2 * GROUP, origin + TILE)
            rest = ref[far, lanes]
            column = lax.broadcasted_iota(jnp.int32, rest.shape, 1)
            among = (column >= base) & (column < base + GROUP)
            after = jnp.zeros((TILE - GROUP - base, TILE), jnp.float32)
            before = [jnp.zeros((base, TILE), jnp.float32)] if base else []
            spread = jnp.concatenate(before + full + [after], axis=0)
            ref[far, lanes] = jnp.where(among, 0.0, rest) - dot32(
                jnp.where(among, rest, 0.0), spread, ((1,), (0,))
            )


def factor_kernel(core, own, other, fields, corr_hbm, out, work, corr, sem):
    first = core[0] == 0

    count = work.shape[0]
    size = out.shape[2]
    pairs = TILE // (2 * size)

    def own_part(k, columns):
        picked = []
        for at in range(k, k + TILE, 2 * size):
            picked.append(
                jnp.where(first, work[at : at + size, columns], work[at + size : at + 2 * size, columns])
            )
        return jnp.concatenate(picked, axis=0)

    def put(k, turned):
        for i in range(pairs):
            for t in range(out.shape[1]):
                out[k // TILE * pairs + i, t] = turned[i * size : (i + 1) * size, t * TILE : (t + 1) * TILE]

    def join():
        for k in range(5):
            rows = slice(k * TILE, (k + 1) * TILE)
            a, b = own[rows, :], other[rows, :]
            for blocks, block in (
                (BLOCKS[0], jnp.where(first, a, b)),
                (BLOCKS[1], jnp.where(first, b, a)),
            ):
                i, j = (slice(t * TILE, (t + 1) * TILE) for t in blocks[k])
                corr[i, j] = block
                if i != j:
                    turned = block.T
                    corr[j, i] = turned
                    work[j, i] = turned
                if j.start or i.start:
                    work[i, j] = block

    def next_tile(k):
        here, after = slice(k, k + TILE), slice(k + TILE, k + 2 * TILE)
        upper = dot32(work[here, here], work[here, after], ((1,), (0,)))
        work[here, after] = upper
        work[after, after] = work[after, after] - dot32(upper.T, upper, ((1,), (0,)))

    def other_tiles(k):
        here = slice(k, k + TILE)
        inverse = work[here, here]
        for side in (slice(k + 2 * TILE, count), slice(0, k)):
            if side.start < side.stop:
                work[here, side] = dot32(inverse, work[here, side], ((1,), (0,)))
        for r in range(k + TILE, count, TILE):
            rows = slice(r, r + TILE)
            lower = work[here, rows].T
            for side in (slice(r + TILE if r == k + TILE else r, count), slice(0, k)):
                if side.start < side.stop:
                    work[rows, side] = work[rows, side] - dot32(lower, work[here, side], ((1,), (0,)))
            work[rows, here] = -dot32(lower, inverse, ((1,), (0,)))
        done = slice(0, k + TILE)
        put(k, dot32(own_part(k, done), fields[done, :], ((1,), (0,))))

    work[0:TILE, 0:TILE] = jnp.where(first, own[0:TILE, :], other[0:TILE, :])
    for k in range(0, count, TILE):
        factor_tile(work, k)
        if k:
            other_tiles(k - TILE)
        else:
            join()
            copy = pltpu.make_async_copy(corr, corr_hbm, sem)
            copy.start()
        if k + TILE < count:
            next_tile(k)
    last = slice(k, count)
    summed = dot32(work[last, 0:k], fields[0:k, :], ((1,), (0,))) + fields[last, :]
    put(k, dot32(own_part(k, last), summed, ((1,), (0,))))
    copy.wait()


VMEM = pl.BlockSpec(memory_space=pltpu.VMEM)
SMEM = pl.BlockSpec(memory_space=pltpu.SMEM)
PARAMS = pltpu.CompilerParams(vmem_limit_bytes=48 << 20)


def flip(axes, bits):
    return [(i, i ^ bits) for i in range(lax.axis_size(axes))]


def per_device(orbitals, potential):
    planes, rows, cells = orbitals.shape
    side = lax.axis_index("xh")
    core = lax.axis_index("c").astype(jnp.int32).reshape(1)
    half = rows // 2
    own, other = (
        jnp.concatenate(
            [lax.dynamic_slice_in_dim(orbitals, at * half, half, 1).reshape(planes * half, cells), potential]
        )
        for at in (side, 1 - side)
    )
    slabs = lax.axis_size(SPACE)
    swap = [(s, s ^ 1) for s in range(slabs)]
    near = [(s, (s + 2 * (2 * (s % 2) - 1)) % slabs) for s in range(slabs)]
    cross = [(s, (s + 2 * (s % 2) - 1) % slabs) for s in range(slabs)]
    cross, swap, near = (
        lax.ppermute(x, SPACE, pairs) for x, pairs in ((other, cross), (other, swap), (own, near))
    )
    second = pl.pallas_call(
        functools.partial(filter_kernel, half, planes),
        out_shape=jax.ShapeDtypeStruct((4 * planes, half, TILE), jnp.float32),
        in_specs=[SMEM] + [VMEM] * 5,
        out_specs=VMEM,
        scratch_shapes=[pltpu.VMEM(((2 * planes + 2 * RADIUS) * half, cells), jnp.float32)],
        compiler_params=PARAMS,
        name="filter",
    )(side.astype(jnp.int32).reshape(1), own, swap, near, cross, jnp.asarray(plane_matrix()))

    team, layer = lax.axis_size(TEAM), lax.axis_size(LAYER)
    mine = lax.all_to_all(second.reshape(layer, 4 * planes // layer, half, TILE), LAYER, 0, 0)
    theirs = lax.ppermute(mine, ("c",), flip("c", 1))
    count = 2 * team * rows
    total = float(planes * lax.axis_size(SPACE) * cells)
    part, fields = pl.pallas_call(
        functools.partial(gram_kernel, 1.0 / total),
        out_shape=(
            jax.ShapeDtypeStruct((5 * TILE, TILE), jnp.float32),
            jax.ShapeDtypeStruct((count, mine.shape[1] * TILE), jnp.float32),
        ),
        in_specs=[SMEM, VMEM, VMEM],
        out_specs=(VMEM, VMEM),
        compiler_params=PARAMS,
        name="gram",
    )(core, mine, theirs)

    piece = lax.all_to_all(part.reshape(layer, 5 * TILE // layer, TILE), LAYER, 0, 0).sum(0)
    depth = lax.axis_size("z")
    piece = lax.all_to_all(jnp.broadcast_to(piece, (depth,) + piece.shape), "z", 0, 0).sum(0)
    spread = lax.all_to_all(jnp.broadcast_to(piece, (layer,) + piece.shape), LAYER, 0, 0)
    mine_g = spread.reshape(5 * TILE, TILE)
    theirs_g = lax.ppermute(mine_g, ("c",), flip("c", 1))
    correlation, turned = pl.pallas_call(
        factor_kernel,
        out_shape=(
            jax.ShapeDtypeStruct((count, count), jnp.float32),
            jax.ShapeDtypeStruct((team, mine.shape[1], rows, TILE), jnp.float32),
        ),
        in_specs=[SMEM, VMEM, VMEM, VMEM],
        out_specs=(pl.BlockSpec(memory_space=pl.ANY), VMEM),
        scratch_shapes=[
            pltpu.VMEM((count, count), jnp.float32),
            pltpu.VMEM((count, count), jnp.float32),
            pltpu.SemaphoreType.DMA,
        ],
        compiler_params=PARAMS,
        name="factor",
    )(core, mine_g, theirs_g, fields)
    back = lax.all_to_all(turned, TEAM, 0, 0).reshape(planes, 2, rows, TILE)
    return (back.transpose(0, 2, 1, 3).reshape(planes, rows, cells), correlation)


def solution(mesh):
    fine = Mesh(mesh.devices.reshape(8, 2, 4, 2, 2), ("z", "xh", "y", "xl", "c"))
    return jax.shard_map(
        per_device,
        mesh=fine,
        in_specs=(P(SPACE, BAND, None), P(SPACE, None)),
        out_specs=(P(SPACE, BAND, None), P()),
        check_vma=False,
    )
```
